128 devices in a mesh: seq: 16 (over x, y), dp: 8 (over z, core).
Axes of the slice: x: 4, y: 4, z: 4, core: 2. Of those that a mesh axis runs over, the one named last changes fastest.
Arguments:
- tokens: bfloat16 [8, 8192, 2048], P('dp', 'seq'), may hold values from -6 to 6
- weights_master: float32 [2048, 3072], P('dp'), may hold values from -0.125 to 0.125
- adam_first: float32 [2048, 3072], P('dp'), may hold values from -6 to 6
- adam_second: float32 [2048, 3072], P('dp'), may hold values from 0.5 to 2
- cotangent: bfloat16 [8, 8192, 1024], P('dp', 'seq'), may hold values from -0.0234375 to 0.0234375
Outputs:
- attended: bfloat16 [8, 8192, 1024], P('dp', 'seq')
- new_weights: float32 [2048, 3072], P('dp')
- new_first: float32 [2048, 3072], P('dp')
- new_second: float32 [2048, 3072], P('dp')
The draws below stay inside these ranges and needn't reach their ends.
All inputs are finite; a program needn't handle non-finite values.
Results may differ from the reference program's by a relative error of at most 0.0035.
The reference program's roundings to bfloat16 on the way count: a program that leaves them out, or rounds other values in their place, can miss the bound.
Values may be sent and summed in bfloat16 or wider, within the bound.
No kernel may reach another device: no remote copies, remote signals or barrier semaphores. Data moves between devices by JAX's collectives and lax.ppermute only.
A program may use at most 128 MiB of HBM per device.

```python
import math
import jax
import jax.numpy as jnp
from jax import lax

D = 2048
HEADS = 8
HDIM = 128
TOK_DEV = 512
BLOCK = 512
STEP = 100
TOKENS = 8192
SEQS = 8
N_SEQ = 16


def spiked(values, rng, source, target, shards_of, factor):
    def block_of(position):
        return (jnp.arange(values.shape[position]) // (values.shape[position] // shards_of)).reshape((-1,) + (1,) * (values.ndim - 1 - position))

    one_side = jax.random.permutation(rng, shards_of)[block_of(target)]
    second = (block_of(target) + shards_of // 2) % shards_of
    return jnp.where((block_of(source) == one_side) | (block_of(source) == second), factor * values, values)


def levels(key, dims, cuts, least, largest):
    level, own = 1.0, jax.random.fold_in(key, 6)
    for dim, blocks in cuts:
        draws = jnp.exp(jax.random.uniform(jax.random.fold_in(own, dim), (blocks,), jnp.float32, least / len(cuts), largest / len(cuts)))
        level = level * jnp.repeat(draws, dims[dim] // blocks).reshape([-1 if axis == dim else 1 for axis in range(len(dims))])
    return level


def centred(key, shape, scale, reach, cuts=(), held_as=jnp.bfloat16):
    array = jax.random.normal(key, shape, jnp.float32) * scale
    if len(cuts) > 0:
        array = levels(key, shape, cuts, -0.22, 0.18) * array
    return jnp.clip(array, min=-reach, max=reach).astype(held_as)


def bell_draw_with(stream_key, shape, spread, reach, shards, heavy, kind=jnp.bfloat16):
    drawn = spread * jax.random.normal(stream_key, shape, jnp.float32)
    if shards:
        drawn = drawn * levels(stream_key, shape, shards, -0.22, 0.18)
    return jnp.clip(spiked(drawn, jax.random.fold_in(stream_key, 3), *heavy), -reach, reach).astype(kind)


def setup_inputs(seed: int = 0) -> dict:
    streams_of = jax.random.split(jax.random.key(seed), 6)
    tokens = bell_draw_with(streams_of[0], (SEQS, TOKENS, D), 1.0, 6.0, ((0, 8), (1, 16)), (0, 2, 8, 2.0))
    weights_master = centred(streams_of[1], (D, 3 * HEADS * HDIM), D ** -0.5, 0.125, ((0, 8),), jnp.float32)
    adam_first = centred(streams_of[2], (D, 3 * HEADS * HDIM), 1.0, 6.0, ((0, 8),), jnp.float32)
    adam_second = jnp.clip(jnp.exp(math.log(2.0) - 1.3862944 * jax.random.uniform(streams_of[3], (D, 3 * HEADS * HDIM), jnp.float32) ** levels(streams_of[3], (D, 3 * HEADS * HDIM), ((0, 8),), -0.2, 0.2)), 0.5, 2.0)
    cotangent = centred(streams_of[4], (SEQS, TOKENS, HEADS * HDIM), (TOKENS * SEQS) ** -0.5, 0.0234375, ((0, 8), (1, 16)))
    return dict(tokens=tokens, weights_master=weights_master, adam_first=adam_first, adam_second=adam_second, cotangent=cotangent)


EPS_NORM = 1e-05
BETA_ONE = 0.9
BETA_TWO = 0.95
LEARN_RATE = 0.001
DECAY_WEIGHT = 0.1
EPS_ADAM = 1e-08

def causal_table():
    places = jnp.arange(BLOCK, dtype=jnp.int32)
    return places[:, None] >= places[None, :]

def block_scores(query_block, key_block):
    causal = causal_table()
    scores = jnp.einsum('the,she->hts', query_block.astype(jnp.float32), key_block.astype(jnp.float32))
    return jnp.where(causal[None], scores, 0.0).astype(jnp.bfloat16)

def forward_block(operands):
    query_block, key_block, value_block, carried_state = operands
    scores = block_scores(query_block, key_block)
    within = jnp.einsum('hts,she->the', scores.astype(jnp.float32), value_block.astype(jnp.float32))
    carried = jnp.einsum('the,hef->thf', query_block.astype(jnp.float32), carried_state.astype(jnp.float32))
    return within + carried

def backward_block(operands):
    query_block, key_block, value_block, grad_block, carried_state, later_state = operands
    causal = causal_table()
    scores = block_scores(query_block, key_block)
    back = jnp.einsum('thf,shf->hts', grad_block.astype(jnp.float32), value_block.astype(jnp.float32))
    back = jnp.where(causal[None], back, 0.0).astype(jnp.bfloat16)
    query_f = query_block.astype(jnp.float32)
    key_f = key_block.astype(jnp.float32)
    value_f = value_block.astype(jnp.float32)
    grad_f = grad_block.astype(jnp.float32)
    carried_f = carried_state.astype(jnp.float32)
    later_f = later_state.astype(jnp.float32)
    back_f = back.astype(jnp.float32)
    scores_f = scores.astype(jnp.float32)
    grad_query = jnp.einsum('hts,she->the', back_f, key_f) + jnp.einsum('thf,hef->the', grad_f, carried_f)
    grad_key = jnp.einsum('hts,the->she', back_f, query_f) + jnp.einsum('shf,hef->she', value_f, later_f)
    grad_value = jnp.einsum('hts,thf->shf', scores_f, grad_f) + jnp.einsum('she,hef->shf', key_f, later_f)
    inner_width = HEADS * HDIM
    joined = jnp.concatenate([grad_query.reshape(BLOCK, inner_width), grad_key.reshape(BLOCK, inner_width), grad_value.reshape(BLOCK, inner_width)], axis=1)
    return joined.astype(jnp.bfloat16)

def sequence_pass(tokens_seq, weights_bf, cotangent_seq):
    blocks = TOKENS // BLOCK
    inner_width = HEADS * HDIM
    qkv = jnp.dot(tokens_seq, weights_bf, preferred_element_type=jnp.float32).astype(jnp.bfloat16)
    queries = qkv[:, :inner_width].reshape(blocks, BLOCK, HEADS, HDIM)
    key_heads = qkv[:, inner_width:2 * inner_width].reshape(blocks, BLOCK, HEADS, HDIM)
    value_heads = qkv[:, 2 * inner_width:].reshape(blocks, BLOCK, HEADS, HDIM)
    kv_local = jnp.einsum('bshe,bshf->bhef', key_heads.astype(jnp.float32), value_heads.astype(jnp.float32))
    prefix_state = (jnp.cumsum(kv_local, 0) - kv_local).astype(jnp.bfloat16)
    mixed = lax.map(forward_block, (queries, key_heads, value_heads, prefix_state))
    inverse_rms = lax.rsqrt(lax.optimization_barrier(jnp.mean(mixed * mixed, -1, keepdims=True)) + EPS_NORM)
    normed = mixed * inverse_rms
    attended_seq = normed.astype(jnp.bfloat16).reshape(TOKENS, inner_width)
    grad_out = cotangent_seq.astype(jnp.float32).reshape(blocks, BLOCK, HEADS, HDIM)
    along = lax.optimization_barrier(jnp.mean(grad_out * normed, -1, keepdims=True))
    grad_mixed = (inverse_rms * (grad_out - normed * along)).astype(jnp.bfloat16)
    qg_local = jnp.einsum('bthe,bthf->bhef', queries.astype(jnp.float32), grad_mixed.astype(jnp.float32))
    suffix_state = (jnp.cumsum(qg_local[::-1], 0)[::-1] - qg_local).astype(jnp.bfloat16)
    grad_qkv = lax.map(backward_block, (queries, key_heads, value_heads, grad_mixed, prefix_state, suffix_state))
    return (attended_seq, grad_qkv.reshape(TOKENS, 3 * inner_width))

def reference(tokens, weights_master, adam_first, adam_second, cotangent):
    weights_bf = weights_master.astype(jnp.bfloat16)

    def one_sequence(running, operands):
        tokens_seq, cotangent_seq = operands
        attended_seq, grad_qkv = sequence_pass(tokens_seq, weights_bf, cotangent_seq)
        device_tokens = tokens_seq.reshape(N_SEQ, TOK_DEV, D)
        device_grads = grad_qkv.reshape(N_SEQ, TOK_DEV, grad_qkv.shape[1])

        def add_device(total, pieces):
            token_rows, grad_rows = pieces
            partial_value = jnp.dot(token_rows.T, grad_rows, preferred_element_type=jnp.float32).astype(jnp.bfloat16)
            partial_value = lax.optimization_barrier(partial_value)
            return (total + partial_value.astype(jnp.float32), None)
        running, unused = lax.scan(add_device, running, (device_tokens, device_grads))
        return (running, attended_seq)
    gradient, attended = lax.scan(one_sequence, jnp.zeros(weights_master.shape, jnp.float32), (tokens, cotangent))
    new_first = BETA_ONE * adam_first + (1.0 - BETA_ONE) * gradient
    new_second = BETA_TWO * adam_second + (1.0 - BETA_TWO) * gradient * gradient
    first_hat = new_first / (1.0 - BETA_ONE ** STEP)
    second_hat = new_second / (1.0 - BETA_TWO ** STEP)
    new_weights = weights_master - LEARN_RATE * (first_hat / (jnp.sqrt(second_hat) + EPS_ADAM) + DECAY_WEIGHT * weights_master)
    return (attended, new_weights, new_first, new_second)
```

```python
import jax
import jax.numpy as jnp
from jax import lax
from jax.experimental import pallas as pl
from jax.experimental.pallas import tpu as pltpu
from jax.sharding import Mesh, PartitionSpec as P


HDIM = 128
BLOCK = 512
STEP = 100
HEADS_CORE = 4

EPS_NORM = 1e-05
BETA_ONE = 0.9
BETA_TWO = 0.95
LEARN_RATE = 0.001
DECAY_WEIGHT = 0.1
EPS_ADAM = 1e-08

BF = jnp.bfloat16
F32 = jnp.float32


PAIRS = {
    "0": [(0, 1), (1, 0), (2, 3), (3, 2)],
    "1": [(1, 2), (2, 1), (3, 0), (0, 3)],
}
CORE_SWAP = [(0, 1), (1, 0)]

GATHER_ORDERS = [("z0", "z1"), ("z1", "z0")]
HALVING = [
    ("x0", "z0", "z1"),
    ("y0", "z1", "z0"),
    ("z0", "x0", "z1"),
    ("z1", "y0", "z0"),
    ("x1", "z0", "z1"),
    ("y1", "z1", "z0"),
]
GROUPS = [
    ((0, 2), ("x1", "y1", "y0"), "x0"),
    ((1, 3), ("y1", "x1", "x0"), "y0"),
    ((4,), ("y0", "x0", "y1"), "x1"),
    ((5,), ("x0", "y0", "x1"), "y1"),
]
WIDTH = HEADS_CORE * HDIM
ROWS = 2 * BLOCK
VMEM = pl.BlockSpec(memory_space=pltpu.VMEM)
barrier = lax.optimization_barrier


def swap(x, dim):
    if dim == "c":
        return lax.ppermute(x, "c", CORE_SWAP)
    return lax.ppermute(x, dim[0], PAIRS[dim[1]])


def gray(place):
    return place ^ (place >> 1)


def place_bit(dim):
    code = gray(lax.axis_index(dim[0]))
    return (code >> int(dim[1])) & 1


def colour():
    return (lax.axis_index("x") + lax.axis_index("y")) & 1


def block_order():
    blocks = []
    for i in range(8):
        code = gray(lax.axis_index("z")) ^ (i >> 2) ^ (((i >> 1) & 1) << 1)
        blocks.append(2 * (code ^ (code >> 1)) + (colour() ^ (i & 1)))
    return jnp.stack(blocks).astype(jnp.int32)


def dot(a, b, ca, cb):
    return lax.dot_general(a, b, (((ca,), (cb,)), ((), ())), preferred_element_type=F32)


def causal(x):
    rows = lax.broadcasted_iota(jnp.int32, x.shape, 0)
    cols = lax.broadcasted_iota(jnp.int32, x.shape, 1)
    return jnp.where(rows >= cols, x, 0.0).astype(BF)


def shape(dims, dtype):
    return jax.ShapeDtypeStruct(dims, dtype)


def prepare_kernel(core, *refs):
    for out, parts in ((refs[7], refs[:3]), (refs[8], refs[3:6])):
        for t in range(HEADS_CORE):
            for u in range(3):
                kind, head = place_of(t, u)
                out[t, :, u * HDIM : (u + 1) * HDIM] = parts[kind][:, cols(head)].astype(BF)
    refs[9][...] = refs[6][...]


def place_of(chunk, slot):
    place = 3 * (chunk % 2) + slot
    return place // 2, 2 * (chunk // 2) + place % 2


def cols(h):
    return slice(h * HDIM, (h + 1) * HDIM)


def prepare(core, master, cot):
    def spec(j, other):
        def index(i, c):
            return i, 2 * j + (1 - c[0] if other else c[0])

        return pl.BlockSpec((128, WIDTH), index)

    out = pl.BlockSpec((HEADS_CORE, 128, 3 * HDIM), lambda i, c: (0, i, 0))
    return pl.pallas_call(
        prepare_kernel,
        name="prepare",
        grid_spec=pltpu.PrefetchScalarGridSpec(
            num_scalar_prefetch=1,
            grid=(2,),
            in_specs=[spec(j, other) for other in (False, True) for j in range(3)]
            + [pl.BlockSpec((256, WIDTH), lambda i, c: (i, 1 - c[0]))],
            out_specs=(out, out, pl.BlockSpec((256, WIDTH), lambda i, c: (i, 0))),
        ),
        out_shape=(shape((HEADS_CORE, 256, 3 * HDIM), BF),) * 2 + (shape((BLOCK, WIDTH), BF),),
    )(core.reshape(1), *([master] * 6), cot)


def arrange_kernel(blocks, own, other, out):
    out[:BLOCK, :] = own[...]
    out[BLOCK:, :] = other[...]


def arrange(blocks, own, other):
    tile = pl.BlockSpec((BLOCK, 256), lambda i, b: (0, b[i]))
    return pl.pallas_call(
        arrange_kernel,
        name="arrange",
        grid_spec=pltpu.PrefetchScalarGridSpec(
            num_scalar_prefetch=1,
            grid=(8,),
            in_specs=[tile, tile],
            out_specs=pl.BlockSpec((ROWS, 256), lambda i, b: (0, i)),
        ),
        out_shape=shape((ROWS, own.shape[1]), BF),
    )(blocks, own, other)


def outer_kernel(keys, values, kv):
    for h in range(2):
        kv[h, 0] = dot(keys[:, cols(h)], values[:, cols(h)], 0, 0)


def project(tokens, pieces):
    chunks = []
    for h, order in enumerate(GATHER_ORDERS):
        mine, low, high = pieces[3 * h : 3 * h + 3]
        theirs = (low, high)
        rows = []
        for i in range(8):
            flips = {"z0": i >> 2, "z1": (i >> 1) & 1}
            place = flips[order[0]] + 2 * flips[order[1]]
            rows.append(theirs[place // 2][place % 2] if i & 1 else mine[place])
        chunks.append(jnp.concatenate(rows, 0))
    weights = jnp.concatenate(chunks, 1)
    qkv = jnp.dot(tokens, weights, preferred_element_type=F32).astype(BF)
    kv = pl.pallas_call(
        outer_kernel,
        name="outer",
        grid=(2,),
        in_specs=[
            pl.BlockSpec((BLOCK, 256), lambda s: (s, 1)),
            pl.BlockSpec((BLOCK, 256), lambda s: (s, 2)),
        ],
        out_specs=pl.BlockSpec((2, 1, HDIM, HDIM), lambda s: (0, s, 0, 0)),
        out_shape=shape((2, 2, HDIM, HDIM), F32),
    )(qkv, qkv)
    return qkv, kv


def lower_scores(a, b):
    low = dot(a[256:], b, 1, 1)
    return causal(dot(a[:256], b[:256], 1, 1)), low[:, :256].astype(BF), causal(low[:, 256:])


def times(scores, x):
    first, left, right = scores
    low = jnp.concatenate([left, right], 1)
    return jnp.concatenate([dot(first, x[:256], 1, 0), dot(low, x, 1, 0)], 0)


def turned_times(scores, x):
    first, left, right = scores
    column = jnp.concatenate([first, left], 0)
    return jnp.concatenate([dot(column, x, 0, 0), dot(right, x[256:], 0, 0)], 0)


def running_kernel(received, out):
    total = jnp.zeros(received.shape[1:], F32)
    for place in range(received.shape[0]):
        out[place] = total.astype(BF)
        total = total + received[place]


def earlier_states(kv):
    cut = kv.reshape(16, -1, HDIM)
    received = lax.all_to_all(cut, ("x", "y"), 0, 0, tiled=True)
    sums = pl.pallas_call(
        running_kernel,
        name="running",
        out_shape=shape(received.shape, BF),
        in_specs=[VMEM],
        out_specs=VMEM,
    )(received)
    return lax.all_to_all(sums, ("x", "y"), 0, 0, tiled=True).reshape(kv.shape)


def heads_of(rows):
    return [tuple(rows[:, cols(2 * j + h)] for j in range(3)) for h in range(2)]


def forward_kernel(core, first, second, state, cot_own, cot_other, attended, grad, qg):
    pair, s = pl.program_id(0), pl.program_id(1)
    cot = jnp.where(s == 0, cot_own[...], cot_other[...])
    for h, (q, k, v) in enumerate(heads_of(jnp.where(pair == 0, first[...], second[...]))):
        mixed = times(lower_scores(q, k), v) + dot(q, state[h, 0], 1, 0)
        inverse = lax.rsqrt(jnp.mean(mixed * mixed, -1, keepdims=True) + EPS_NORM)
        normed = mixed * inverse
        attended[:, cols(h)] = normed.astype(BF)
        out_grad = cot[:, cols(h)].astype(F32)
        along = jnp.mean(out_grad * normed, -1, keepdims=True)
        g = (inverse * (out_grad - normed * along)).astype(BF)
        grad[:, cols(h)] = g
        qg[h, 0] = dot(q, g, 0, 0).astype(BF)


def forward(core, first, second, state, cot_own, cot_other):
    rows = pl.BlockSpec((BLOCK, 256), lambda p, s, c: (s, p))
    states = pl.BlockSpec((2, 1, HDIM, HDIM), lambda p, s, c: (p, s, 0, 0))
    qkv_rows = (BLOCK, 6 * HDIM)
    return pl.pallas_call(
        forward_kernel,
        name="forward",
        grid_spec=pltpu.PrefetchScalarGridSpec(
            num_scalar_prefetch=1,
            grid=(2, 2),
            in_specs=[
                pl.BlockSpec(qkv_rows, lambda p, s, c: (jnp.where(p == 0, s, 1), 0)),
                pl.BlockSpec(qkv_rows, lambda p, s, c: (jnp.where(p == 0, 0, s), 0)),
                states,
                pl.BlockSpec((BLOCK, 256), lambda p, s, c: (0, 2 * c[0] + p)),
                pl.BlockSpec((BLOCK, 256), lambda p, s, c: (0, p)),
            ],
            out_specs=(rows, rows, states),
        ),
        out_shape=(
            shape((ROWS, WIDTH), BF),
            shape((ROWS, WIDTH), BF),
            shape((HEADS_CORE, 2, HDIM, HDIM), BF),
        ),
    )(core.reshape(1), first, second, state, cot_own, cot_other)


def backward_kernel(qkv, grad, state, dq, dk, dv):
    for h, (q, k, v) in enumerate(heads_of(qkv[...])):
        g = grad[:, cols(h)]
        back = lower_scores(g, v)
        dq[:, cols(h)] = (times(back, k) + dot(g, state[h, 0], 1, 1)).astype(BF)
        dk[:, cols(h)] = turned_times(back, q)
        dv[:, cols(h)] = turned_times(lower_scores(q, k), g)


def backward(pair, qkv, grad, state):
    rows = pl.BlockSpec((BLOCK, 256), lambda s: (s, 0))
    return pl.pallas_call(
        backward_kernel,
        grid=(2,),
        in_specs=[
            pl.BlockSpec((BLOCK, 6 * HDIM), lambda s: (s, 0)),
            pl.BlockSpec((BLOCK, 256), lambda s: (s, pair)),
            pl.BlockSpec((2, 1, HDIM, HDIM), lambda s: (pair, s, 0, 0)),
        ],
        out_specs=(rows, rows, rows),
        out_shape=(shape((ROWS, 256), BF), shape((ROWS, 256), F32), shape((ROWS, 256), F32)),
    )(qkv, grad, state)


def later_kernel(first, second, dk0, dk1, dv0, dv1, state, dk, dv):
    for pair, (qkv, dk_in, dv_in) in enumerate(((first, dk0, dv0), (second, dk1, dv1))):
        for h, (_, k, v) in enumerate(heads_of(qkv)):
            head = 2 * pair + h
            later = state[head, 0]
            dk[:, cols(head)] = (dk_in[:, cols(h)] + dot(v, later, 1, 1)).astype(BF)
            dv[:, cols(head)] = (dv_in[:, cols(h)] + dot(k, later, 1, 0)).astype(BF)


def add_later(first, second, dk, dv, state):
    def rows(width):
        return pl.BlockSpec((BLOCK, width), lambda s: (s, 0))

    states = pl.BlockSpec((HEADS_CORE, 1, HDIM, HDIM), lambda s: (0, s, 0, 0))
    return pl.pallas_call(
        later_kernel,
        name="later",
        grid=(2,),
        in_specs=[rows(6 * HDIM)] * 2 + [rows(256)] * 4 + [states],
        out_specs=(rows(WIDTH), rows(WIDTH)),
        out_shape=(shape((ROWS, WIDTH), BF),) * 2,
    )(first, second, *dk, *dv, state)


def partial_gradient(tokens, grads):
    partial = dot(tokens, grads, 0, 0).astype(BF).reshape(2, 2, 2, 256, WIDTH)
    return partial[..., :256], partial[..., 256:]


def wide(x):
    return x.astype(F32)


def add(a, b):
    return (wide(a) + wide(b)).astype(BF)


def reduce_part(part, order):
    left = ["z0", "z1", "flat"]
    for dim in order:
        name = dim if dim[0] == "z" else "flat"
        axis = left.index(name)
        left.remove(name)
        if name == "flat":
            keeps = colour() ^ place_bit(dim)
            send = lax.dynamic_index_in_dim(part, 1 - keeps, axis, False)
            keep = lax.dynamic_index_in_dim(part, keeps, axis, False)
        else:
            send = lax.index_in_dim(part, 1, axis, False)
            keep = lax.index_in_dim(part, 0, axis, False)
        part = add(keep, swap(send, dim))
    return part


def finish_group(parts, exchanged, last):
    total = jnp.stack(parts)
    for dim in exchanged:
        total = add(total, swap(total, dim))
    return total, swap(total, last)


def later_steps(total, later):
    total = wide(total)
    carried = jnp.zeros_like(total)
    for dim in ("y0", "y1", "x0", "x1"):
        received = yield swap(total.astype(BF), dim)
        received = wide(received)
        upper = (lax.axis_index(dim[0]) >> int(dim[1])) & 1
        carried = carried + jnp.where(upper == (0 if later else 1), received, 0.0)
        total = total + received
    yield carried.astype(BF)


def gather_step(step, mine):
    got = []
    for h in range(2):
        got.append(swap(mine[h], GATHER_ORDERS[h][step]))
    return [jnp.concatenate([mine[h], got[h]], 0) for h in range(2)]


def exchange_colours(mine):
    pieces = []
    for h, axis in enumerate("xy"):
        pieces.append(mine[h])
        for side in range(2):
            pieces.append(swap(mine[h][2 * side : 2 * side + 2], f"{axis}{side}"))
    return pieces


def step(tokens, weights_master, adam_first, adam_second, cotangent):
    core = lax.axis_index("c")
    own = tokens[0]
    straight = colour() == core

    held, outgoing, cot_out = prepare(core, weights_master, cotangent[0])
    traded = swap(outgoing, "c")
    other = swap(own, "c")
    cot_other = swap(cot_out, "c")

    blocks = block_order()
    mine = jnp.where(straight, held, traded)
    first = gather_step(0, [mine[0][None], mine[1][None]])
    first = gather_step(1, first)
    both = arrange(blocks, own, other)
    first, mine, both = barrier((first, mine, both))
    pieces = exchange_colours(first)
    second = gather_step(0, [mine[2][None], mine[3][None]])
    second = gather_step(1, second)
    qkv_first, kv_first = project(both, pieces)
    second, qkv_first, kv_first = barrier((second, qkv_first, kv_first))
    qkv_second, kv_second = project(both, exchange_colours(second))

    state = earlier_states(jnp.concatenate([kv_first, kv_second], 0))
    attended, grad, qg = forward(core, qkv_first, qkv_second, state, cotangent[0], cot_other)

    steps = later_steps(qg, True)
    received = next(steps)
    q0, k0, v0 = backward(0, qkv_first, grad, state)
    received, q0, k0, v0, grad = barrier((received, q0, k0, v0, grad))
    received = steps.send(received)
    q1, k1, v1 = backward(1, qkv_second, grad, state)
    received, q0, q1, k1, v1 = barrier((received, q0, q1, k1, v1))
    received = steps.send(received)
    parts = list(partial_gradient(both, jnp.concatenate([q0, q1], 1)))
    received, parts = barrier((received, parts))
    received = steps.send(received)
    later = steps.send(received)
    dk, dv = add_later(qkv_first, qkv_second, (k0, k1), (v0, v1), later)
    parts += list(partial_gradient(both, dk))
    parts += list(partial_gradient(both, dv))

    attended_other = swap(attended[BLOCK:], "c")
    low = jnp.where(core == 0, attended[:BLOCK], attended_other)
    high = jnp.where(core == 0, attended_other, attended[:BLOCK])
    attended_out = jnp.concatenate([low, high], 1)[None]

    reduced = [reduce_part(part, order) for part, order in zip(parts, HALVING)]
    kept, sent = [None] * 6, [None] * 6
    for members, exchanged, last in GROUPS:
        here, there = finish_group([reduced[p] for p in members], exchanged, last)
        holds = place_bit(last) == core
        for i, p in enumerate(members):
            kept[p] = jnp.where(holds, here[i], there[i])
            sent[p] = jnp.where(holds, there[i], here[i])
    received = swap(jnp.stack(sent), "c")
    pieces = []
    for g in range(3):
        a = jnp.concatenate([kept[2 * g], kept[2 * g + 1]], 1)
        b = jnp.concatenate([received[2 * g], received[2 * g + 1]], 1)
        pieces += [jnp.where(core == 0, a, b), jnp.where(core == 0, b, a)]
    gradient = jnp.concatenate(pieces, 1).astype(F32)

    new_first = BETA_ONE * adam_first + (1.0 - BETA_ONE) * gradient
    new_second = BETA_TWO * adam_second + (1.0 - BETA_TWO) * gradient * gradient
    first_hat = new_first / (1.0 - BETA_ONE**STEP)
    second_hat = new_second / (1.0 - BETA_TWO**STEP)
    new_weights = weights_master - LEARN_RATE * (
        first_hat / (jnp.sqrt(second_hat) + EPS_ADAM) + DECAY_WEIGHT * weights_master
    )
    return (attended_out, new_weights, new_first, new_second)


def solution(mesh):
    torus = Mesh(mesh.devices.reshape(4, 4, 4, 2), ("x", "y", "z", "c"))
    rows = P(("z", "c"), ("x", "y"), None)
    shard = P(("z", "c"), None)
    return jax.shard_map(
        step,
        mesh=torus,
        in_specs=(rows, shard, shard, shard, rows),
        out_specs=(rows, shard, shard, shard),
        check_vma=False,
    )
```

```python
import jax
import jax.numpy as jnp
from jax import lax
from jax.experimental import pallas as pl
from jax.experimental.pallas import tpu as pltpu
from jax.sharding import Mesh, PartitionSpec as P


HDIM = 128
BLOCK = 512
STEP = 100
HEADS_CORE = 4

EPS_NORM = 1e-05
BETA_ONE = 0.9
BETA_TWO = 0.95
LEARN_RATE = 0.001
DECAY_WEIGHT = 0.1
EPS_ADAM = 1e-08

BF = jnp.bfloat16
F32 = jnp.float32


PAIRS = {
    "0": [(0, 1), (1, 0), (2, 3), (3, 2)],
    "1": [(1, 2), (2, 1), (3, 0), (0, 3)],
}
CORE_SWAP = [(0, 1), (1, 0)]

GATHER_ORDERS = [("z0", "z1"), ("z1", "z0")]
HALVING = [
    ("x0", "z0", "z1"),
    ("y0", "z1", "z0"),
    ("z0", "x0", "z1"),
    ("z1", "y0", "z0"),
    ("x1", "z0", "z1"),
    ("y1", "z1", "z0"),
]
GROUPS = [
    ((0, 2), ("x1", "y1", "y0"), "x0"),
    ((1, 3), ("y1", "x1", "x0"), "y0"),
    ((4,), ("y0", "x0", "y1"), "x1"),
    ((5,), ("x0", "y0", "x1"), "y1"),
]
WIDTH = HEADS_CORE * HDIM
ROWS = 2 * BLOCK
VMEM = pl.BlockSpec(memory_space=pltpu.VMEM)
barrier = lax.optimization_barrier


def swap(x, dim):
    if dim == "c":
        return lax.ppermute(x, "c", CORE_SWAP)
    return lax.ppermute(x, dim[0], PAIRS[dim[1]])


def gray(place):
    return place ^ (place >> 1)


def place_bit(dim):
    code = gray(lax.axis_index(dim[0]))
    return (code >> int(dim[1])) & 1


def colour():
    return (lax.axis_index("x") + lax.axis_index("y")) & 1


def block_order():
    blocks = []
    for i in range(8):
        code = gray(lax.axis_index("z")) ^ (i >> 2) ^ (((i >> 1) & 1) << 1)
        blocks.append(2 * (code ^ (code >> 1)) + (colour() ^ (i & 1)))
    return jnp.stack(blocks).astype(jnp.int32)


def dot(a, b, ca, cb):
    return lax.dot_general(a, b, (((ca,), (cb,)), ((), ())), preferred_element_type=F32)


def causal(x):
    rows = lax.broadcasted_iota(jnp.int32, x.shape, 0)
    cols = lax.broadcasted_iota(jnp.int32, x.shape, 1)
    return jnp.where(rows >= cols, x, 0.0).astype(BF)


def shape(dims, dtype):
    return jax.ShapeDtypeStruct(dims, dtype)


def prepare_kernel(core, *refs):
    for out, parts in ((refs[7], refs[:3]), (refs[8], refs[3:6])):
        for t in range(HEADS_CORE):
            for u in range(3):
                kind, head = place_of(t, u)
                out[t, :, u * HDIM : (u + 1) * HDIM] = parts[kind][:, cols(head)].astype(BF)
    refs[9][...] = refs[6][...]


def place_of(chunk, slot):
    place = 3 * (chunk % 2) + slot
    return place // 2, 2 * (chunk // 2) + place % 2


def cols(h):
    return slice(h * HDIM, (h + 1) * HDIM)


def prepare(core, master, cot):
    def spec(j, other):
        def index(i, c):
            return i, 2 * j + (1 - c[0] if other else c[0])

        return pl.BlockSpec((128, WIDTH), index)

    out = pl.BlockSpec((HEADS_CORE, 128, 3 * HDIM), lambda i, c: (0, i, 0))
    return pl.pallas_call(
        prepare_kernel,
        name="prepare",
        grid_spec=pltpu.PrefetchScalarGridSpec(
            num_scalar_prefetch=1,
            grid=(2,),
            in_specs=[spec(j, other) for other in (False, True) for j in range(3)]
            + [pl.BlockSpec((256, WIDTH), lambda i, c: (i, 1 - c[0]))],
            out_specs=(out, out, pl.BlockSpec((256, WIDTH), lambda i, c: (i, 0))),
        ),
        out_shape=(shape((HEADS_CORE, 256, 3 * HDIM), BF),) * 2 + (shape((BLOCK, WIDTH), BF),),
    )(core.reshape(1), *([master] * 6), cot)


def arrange_kernel(blocks, own, other, out):
    out[:BLOCK, :] = own[...]
    out[BLOCK:, :] = other[...]


def arrange(blocks, own, other):
    tile = pl.BlockSpec((BLOCK, 256), lambda i, b: (0, b[i]))
    return pl.pallas_call(
        arrange_kernel,
        name="arrange",
        grid_spec=pltpu.PrefetchScalarGridSpec(
            num_scalar_prefetch=1,
            grid=(8,),
            in_specs=[tile, tile],
            out_specs=pl.BlockSpec((ROWS, 256), lambda i, b: (0, i)),
        ),
        out_shape=shape((ROWS, own.shape[1]), BF),
    )(blocks, own, other)


def outer_kernel(pair, keys, values, before, kv):
    for h in range(2):
        kv[h, 0] = dot(keys[:, cols(h)], values[:, cols(h)], 0, 0)


def project(pair, tokens, pieces, before):
    chunks = []
    for h, order in enumerate(GATHER_ORDERS):
        mine, low, high = pieces[3 * h : 3 * h + 3]
        theirs = (low, high)
        rows = []
        for i in range(8):
            flips = {"z0": i >> 2, "z1": (i >> 1) & 1}
            place = flips[order[0]] + 2 * flips[order[1]]
            rows.append(theirs[place // 2][place % 2] if i & 1 else mine[place])
        chunks.append(jnp.concatenate(rows, 0))
    weights = jnp.concatenate(chunks, 1)
    qkv = jnp.dot(tokens, weights, preferred_element_type=F32).astype(BF)
    kv = pl.pallas_call(
        outer_kernel,
        name="outer",
        grid_spec=pltpu.PrefetchScalarGridSpec(
            num_scalar_prefetch=1,
            grid=(2,),
            in_specs=[
                pl.BlockSpec((BLOCK, 256), lambda s, p: (s, 1)),
                pl.BlockSpec((BLOCK, 256), lambda s, p: (s, 2)),
                pl.BlockSpec(memory_space=pl.ANY),
            ],
            out_specs=pl.BlockSpec((2, 1, HDIM, HDIM), lambda s, p: (p[0], s, 0, 0)),
        ),
        out_shape=shape((HEADS_CORE, 2, HDIM, HDIM), F32),
        input_output_aliases={3: 0},
    )(jnp.full((1,), pair, jnp.int32), qkv, qkv, before)
    return qkv, kv


def lower_scores(a, b):
    low = dot(a[256:], b, 1, 1)
    return causal(dot(a[:256], b[:256], 1, 1)), low[:, :256].astype(BF), causal(low[:, 256:])


def times(scores, x):
    first, left, right = scores
    low = jnp.concatenate([left, right], 1)
    return jnp.concatenate([dot(first, x[:256], 1, 0), dot(low, x, 1, 0)], 0)


def turned_times(scores, x):
    first, left, right = scores
    column = jnp.concatenate([first, left], 0)
    return jnp.concatenate([dot(column, x, 0, 0), dot(right, x[256:], 0, 0)], 0)


def running_kernel(received, out):
    total = jnp.zeros(received.shape[1:], F32)
    for place in range(received.shape[0]):
        out[place] = total.astype(BF)
        total = total + received[place]


def earlier_states(kv):
    cut = kv.reshape(16, -1, HDIM)
    received = lax.all_to_all(cut, ("x", "y"), 0, 0, tiled=True)
    sums = pl.pallas_call(
        running_kernel,
        name="running",
        out_shape=shape(received.shape, BF),
        in_specs=[VMEM],
        out_specs=VMEM,
    )(received)
    return lax.all_to_all(sums, ("x", "y"), 0, 0, tiled=True).reshape(kv.shape)


def head_of(ref, h, kind):
    return ref[:, pl.ds(pl.multiple_of((2 * "qkv".index(kind) + h) * HDIM, HDIM), HDIM)]


def head_cols(h):
    return pl.ds(pl.multiple_of(h * HDIM, HDIM), HDIM)


def each_head(body):
    def one(h, carry):
        body(h)
        return carry

    lax.fori_loop(0, 2, one, 0)


def pair_specs():
    qkv_rows = (BLOCK, 6 * HDIM)
    return [
        pl.BlockSpec(qkv_rows, lambda p, s, *_: (jnp.where(p == 0, s, 1), 0)),
        pl.BlockSpec(qkv_rows, lambda p, s, *_: (jnp.where(p == 0, 0, s), 0)),
    ]


def head_rows():
    return pl.BlockSpec((BLOCK, 256), lambda p, s, *_: (s, p))


def pick(first, second, h, kinds):
    pair = pl.program_id(0)
    return [jnp.where(pair == 0, head_of(first, h, j), head_of(second, h, j)) for j in kinds]


def within_kernel(first, second, out):
    @each_head
    def _(h):
        q, k, v = pick(first, second, h, "qkv")
        out[:, head_cols(h)] = times(lower_scores(q, k), v)


def local_scores(first, second):
    return pl.pallas_call(
        within_kernel,
        name="within",
        grid=(2, 2),
        in_specs=pair_specs(),
        out_specs=head_rows(),
        out_shape=shape((ROWS, WIDTH), F32),
    )(first, second)


def forward_kernel(core, first, second, within, state, cot_own, cot_other, attended, grad, qg):
    s = pl.program_id(1)

    @each_head
    def _(h):
        (q,) = pick(first, second, h, "q")
        at = head_cols(h)
        mixed = within[:, at] + dot(q, state[h, 0], 1, 0)
        inverse = lax.rsqrt(jnp.mean(mixed * mixed, -1, keepdims=True) + EPS_NORM)
        normed = mixed * inverse
        attended[:, at] = normed.astype(BF)
        out_grad = jnp.where(s == 0, cot_own[:, at], cot_other[:, at]).astype(F32)
        along = jnp.mean(out_grad * normed, -1, keepdims=True)
        g = (inverse * (out_grad - normed * along)).astype(BF)
        grad[:, at] = g
        qg[h, 0] = dot(q, g, 0, 0).astype(BF)


def forward(core, first, second, within, state, cot_own, cot_other):
    rows = head_rows()
    states = pl.BlockSpec((2, 1, HDIM, HDIM), lambda p, s, c: (p, s, 0, 0))
    queries = (BLOCK, 2 * HDIM)
    return pl.pallas_call(
        forward_kernel,
        name="forward",
        grid_spec=pltpu.PrefetchScalarGridSpec(
            num_scalar_prefetch=1,
            grid=(2, 2),
            in_specs=[
                pl.BlockSpec(queries, lambda p, s, c: (jnp.where(p == 0, s, 1), 0)),
                pl.BlockSpec(queries, lambda p, s, c: (jnp.where(p == 0, 0, s), 0)),
                rows,
                states,
                pl.BlockSpec((BLOCK, 256), lambda p, s, c: (0, 2 * c[0] + p)),
                pl.BlockSpec((BLOCK, 256), lambda p, s, c: (0, p)),
            ],
            out_specs=(rows, rows, states),
        ),
        out_shape=(
            shape((ROWS, WIDTH), BF),
            shape((ROWS, WIDTH), BF),
            shape((HEADS_CORE, 2, HDIM, HDIM), BF),
        ),
    )(core.reshape(1), first, second, within, state, cot_own, cot_other)


def backward_kernel(pair, qkv, grad, state, dq, dkv):
    @each_head
    def _(h):
        q, k, v = [head_of(qkv, h, j) for j in "qkv"]
        at = head_cols(h)
        g = grad[:, at]
        back = lower_scores(g, v)
        dq[:, at] = (times(back, k) + dot(g, state[h, 0], 1, 1)).astype(BF)
        dkv[0, :, at] = turned_times(back, q)
        dkv[1, :, at] = turned_times(lower_scores(q, k), g)


def backward(pair, qkv, grad, state):
    return pl.pallas_call(
        backward_kernel,
        name="backward",
        grid_spec=pltpu.PrefetchScalarGridSpec(
            num_scalar_prefetch=1,
            grid=(2,),
            in_specs=[
                pl.BlockSpec((BLOCK, 6 * HDIM), lambda s, p: (s, 0)),
                pl.BlockSpec((BLOCK, 256), lambda s, p: (s, p[0])),
                pl.BlockSpec((2, 1, HDIM, HDIM), lambda s, p: (p[0], s, 0, 0)),
            ],
            out_specs=(
                pl.BlockSpec((BLOCK, 256), lambda s, p: (s, 0)),
                pl.BlockSpec((2, BLOCK, 256), lambda s, p: (0, s, 0)),
            ),
        ),
        out_shape=(shape((ROWS, 256), BF), shape((2, ROWS, 256), F32)),
    )(jnp.full((1,), pair, jnp.int32), qkv, grad, state)


def multiply_blocks(turned, tokens, out):
    def block(i, carry):
        at = pl.ds(pl.multiple_of(i * 256, 256), 256)
        piece = dot(turned[...], tokens[:, at], 1, 0).astype(BF)
        out[0, 0, i] = piece[:256]
        out[0, 1, i] = piece[256:]
        return carry

    lax.fori_loop(0, tokens.shape[1] // 256, block, 0)


def query_gradient_kernel(q0, q1, tokens, out, turned):
    turned[:256, :] = q0[...].T
    turned[256:, :] = q1[...].T
    multiply_blocks(turned, tokens, out)


def gradient_kernel(first, second, d_first, d_second, state, tokens, out, turned):
    kind = pl.program_id(0)
    for pair, (rows, within) in enumerate(((first, d_first), (second, d_second))):

        @each_head
        def _(h):
            head = 2 * pair + h
            at = head_cols(h)
            for s in range(2):
                span = slice(s * BLOCK, (s + 1) * BLOCK)
                later = state[head, s]
                later = jnp.where(kind == 0, later.T, later)
                total = within[0, span, at] + dot(rows[span, at], later, 1, 0)
                turned[head_cols(head), span] = total.astype(BF).T

    multiply_blocks(turned, tokens, out)


def gradient_call(kernel, count, ins, specs, tokens):
    blocks = tokens.shape[1] // 256
    return pl.pallas_call(
        kernel,
        grid=(count,),
        in_specs=specs + [VMEM],
        out_specs=pl.BlockSpec((1, 2, blocks, 256, 256), lambda j: (j, 0, 0, 0, 0)),
        out_shape=shape((count, 2, blocks, 256, 256), BF),
        scratch_shapes=[pltpu.VMEM((WIDTH, ROWS), BF)],
    )(*ins, tokens)


def query_gradient(q0, q1, tokens):
    return gradient_call(query_gradient_kernel, 1, (q0, q1), [VMEM] * 2, tokens)


def key_value_gradient(first, second, d_first, d_second, state, tokens):
    rows = pl.BlockSpec((ROWS, 256), lambda j: (0, 2 - j))
    within = pl.BlockSpec((1, ROWS, 256), lambda j: (j, 0, 0))
    specs = [rows, rows, within, within, VMEM]
    ins = (first, second, d_first, d_second, state)
    return gradient_call(gradient_kernel, 2, ins, specs, tokens)


def parts_of(partial):
    return [
        partial[j, i].reshape(2, 2, 2, 256, 256) for j in range(partial.shape[0]) for i in range(2)
    ]


def wide(x):
    return x.astype(F32)


def add(a, b):
    return (wide(a) + wide(b)).astype(BF)


def reduce_part(part, order):
    left = ["z0", "z1", "flat"]
    for dim in order:
        name = dim if dim[0] == "z" else "flat"
        axis = left.index(name)
        left.remove(name)
        if name == "flat":
            keeps = colour() ^ place_bit(dim)
            send = lax.dynamic_index_in_dim(part, 1 - keeps, axis, False)
            keep = lax.dynamic_index_in_dim(part, keeps, axis, False)
        else:
            send = lax.index_in_dim(part, 1, axis, False)
            keep = lax.index_in_dim(part, 0, axis, False)
        part = add(keep, swap(send, dim))
    return part


def finish_group(parts, exchanged, last):
    total = jnp.stack(parts)
    for dim in exchanged:
        total = add(total, swap(total, dim))
    return total, swap(total, last)


def later_steps(total, later):
    total = wide(total)
    carried = jnp.zeros_like(total)
    for dim in ("y0", "y1", "x0", "x1"):
        received = yield swap(total.astype(BF), dim)
        received = wide(received)
        upper = (lax.axis_index(dim[0]) >> int(dim[1])) & 1
        carried = carried + jnp.where(upper == (0 if later else 1), received, 0.0)
        total = total + received
    yield carried.astype(BF)


def sort_kernel(holds, *refs):
    kept, sent = refs[-2:]

    def rows(i, carry):
        at = pl.ds(pl.multiple_of(i * 64, 64), 64)
        for g, (members, _, _) in enumerate(GROUPS):
            straight = holds[g] == 1
            for j, p in enumerate(members):
                here, there = refs[2 * g][j, at, :], refs[2 * g + 1][j, at, :]
                kept[p, at, :] = jnp.where(straight, here, there)
                sent[p, at, :] = jnp.where(straight, there, here)
        return carry

    lax.fori_loop(0, 4, rows, 0)


def sort_pieces(holds, finished):
    return pl.pallas_call(
        sort_kernel,
        name="sort_pieces",
        in_specs=[pl.BlockSpec(memory_space=pltpu.SMEM)] + [VMEM] * len(finished),
        out_specs=(VMEM, VMEM),
        out_shape=(shape((6, 256, 256), BF),) * 2,
    )(holds, *finished)


def adam_kernel(core, kept, received, weights, first, second, out_weights, out_first, out_second):
    straight = (pl.program_id(0) // 2) % 2 == core[0]
    gradient = jnp.where(straight, kept[0], received[0]).astype(F32).T
    new_first = BETA_ONE * first[...] + (1.0 - BETA_ONE) * gradient
    new_second = BETA_TWO * second[...] + (1.0 - BETA_TWO) * gradient * gradient
    first_hat = new_first / (1.0 - BETA_ONE**STEP)
    second_hat = new_second / (1.0 - BETA_TWO**STEP)
    out_first[...] = new_first
    out_second[...] = new_second
    out_weights[...] = weights[...] - LEARN_RATE * (
        first_hat / (jnp.sqrt(second_hat) + EPS_ADAM) + DECAY_WEIGHT * weights[...]
    )


def adam(core, kept, received, *arrays):
    piece = pl.BlockSpec((1, 256, 256), lambda n, c: (2 * (n // 4) + n % 2, 0, 0))
    block = pl.BlockSpec((256, 256), lambda n, c: (0, n))
    return pl.pallas_call(
        adam_kernel,
        name="adam",
        grid_spec=pltpu.PrefetchScalarGridSpec(
            num_scalar_prefetch=1,
            grid=(12,),
            in_specs=[piece, piece, block, block, block],
            out_specs=(block,) * 3,
        ),
        out_shape=tuple(shape(x.shape, F32) for x in arrays),
    )(core.reshape(1), kept, received, *arrays)


def gather_step(step, mine):
    got = []
    for h in range(2):
        got.append(swap(mine[h], GATHER_ORDERS[h][step]))
    return [jnp.concatenate([mine[h], got[h]], 0) for h in range(2)]


def exchange_colours(mine):
    pieces = []
    for h, axis in enumerate("xy"):
        pieces.append(mine[h])
        for side in range(2):
            pieces.append(swap(mine[h][2 * side : 2 * side + 2], f"{axis}{side}"))
    return pieces


def step(tokens, weights_master, adam_first, adam_second, cotangent):
    core = lax.axis_index("c")
    own = tokens[0]
    straight = colour() == core

    held, outgoing, cot_out = prepare(core, weights_master, cotangent[0])
    traded = swap(outgoing, "c")
    other = swap(own, "c")
    cot_other = swap(cot_out, "c")

    blocks = block_order()
    mine = jnp.where(straight, held, traded)
    first = gather_step(0, [mine[0][None], mine[1][None]])
    first = gather_step(1, first)
    both = arrange(blocks, own, other)
    first, mine, both = barrier((first, mine, both))
    pieces = exchange_colours(first)
    second = gather_step(0, [mine[2][None], mine[3][None]])
    second = gather_step(1, second)
    kv = jnp.zeros((HEADS_CORE, 2, HDIM, HDIM), F32)
    qkv_first, kv = project(0, both, pieces, kv)
    second, qkv_first, kv = barrier((second, qkv_first, kv))
    qkv_second, kv = project(1, both, exchange_colours(second), kv)

    state = earlier_states(kv)
    within = local_scores(qkv_first, qkv_second)
    attended, grad, qg = forward(
        core, qkv_first, qkv_second, within, state, cotangent[0], cot_other
    )

    steps = later_steps(qg, True)
    received = next(steps)
    q0, d0 = backward(0, qkv_first, grad, state)
    received, q0, d0, grad = barrier((received, q0, d0, grad))
    received = steps.send(received)
    q1, d1 = backward(1, qkv_second, grad, state)
    received, q0, q1, d1 = barrier((received, q0, q1, d1))
    received = steps.send(received)
    parts = parts_of(query_gradient(q0, q1, both))
    received, parts = barrier((received, parts))
    received = steps.send(received)
    later = steps.send(received)
    parts += parts_of(key_value_gradient(qkv_first, qkv_second, d0, d1, later, both))

    attended_other = swap(attended[BLOCK:], "c")
    low = jnp.where(core == 0, attended[:BLOCK], attended_other)
    high = jnp.where(core == 0, attended_other, attended[:BLOCK])
    attended_out = jnp.concatenate([low, high], 1)[None]

    reduced = [reduce_part(part, order) for part, order in zip(parts, HALVING)]
    holds, finished = [], []
    for members, exchanged, last in GROUPS:
        holds.append(place_bit(last) == core)
        finished += finish_group([reduced[p] for p in members], exchanged, last)
    kept, sent = sort_pieces(jnp.stack(holds).astype(jnp.int32), finished)
    received = swap(sent, "c")
    new_weights, new_first, new_second = adam(
        core, kept, received, weights_master, adam_first, adam_second
    )
    return (attended_out, new_weights, new_first, new_second)


def solution(mesh):
    torus = Mesh(mesh.devices.reshape(4, 4, 4, 2), ("x", "y", "z", "c"))
    rows = P(("z", "c"), ("x", "y"), None)
    shard = P(("z", "c"), None)
    return jax.shard_map(
        step,
        mesh=torus,
        in_specs=(rows, shard, shard, shard, rows),
        out_specs=(rows, shard, shard, shard),
        check_vma=False,
    )
```

```python
import functools

import jax
import jax.numpy as jnp
from jax import lax
from jax.experimental import pallas as pl
from jax.experimental.pallas import tpu as pltpu
from jax.sharding import Mesh, PartitionSpec as P


HDIM = 128
BLOCK = 512
STEP = 100
HEADS_CORE = 4

EPS_NORM = 1e-05
BETA_ONE = 0.9
BETA_TWO = 0.95
LEARN_RATE = 0.001
DECAY_WEIGHT = 0.1
EPS_ADAM = 1e-08

BF = jnp.bfloat16
F32 = jnp.float32


PAIRS = {
    "0": [(0, 1), (1, 0), (2, 3), (3, 2)],
    "1": [(1, 2), (2, 1), (3, 0), (0, 3)],
}
CORE_SWAP = [(0, 1), (1, 0)]

GATHER_ORDERS = [("z0", "z1"), ("z1", "z0")]
HALVING = [
    ("x0", "z0", "z1"),
    ("y0", "z1", "z0"),
    ("x0", "z0", "z1"),
    ("y0", "z1", "z0"),
    ("x1", "z0", "z1"),
    ("y1", "z1", "z0"),
]
GROUPS = [
    ((0, 2), ("x1", "y1", "y0"), "x0"),
    ((1, 3), ("y1", "x1", "x0"), "y0"),
    ((4,), ("y0", "x0", "y1"), "x1"),
    ((5,), ("x0", "y0", "x1"), "y1"),
]
WIDTH = HEADS_CORE * HDIM
ROWS = 2 * BLOCK
VMEM = pl.BlockSpec(memory_space=pltpu.VMEM)
barrier = lax.optimization_barrier


def swap(x, dim):
    if dim == "c":
        return lax.ppermute(x, "c", CORE_SWAP)
    return lax.ppermute(x, dim[0], PAIRS[dim[1]])


def gray(place):
    return place ^ (place >> 1)


def place_bit(dim):
    code = gray(lax.axis_index(dim[0]))
    return (code >> int(dim[1])) & 1


def colour():
    return (lax.axis_index("x") + lax.axis_index("y")) & 1


def block_order():
    blocks = []
    for i in range(8):
        code = gray(lax.axis_index("z")) ^ (i >> 2) ^ (((i >> 1) & 1) << 1)
        blocks.append(2 * (code ^ (code >> 1)) + (colour() ^ (i & 1)))
    return jnp.stack(blocks).astype(jnp.int32)


def dot(a, b, ca, cb):
    return lax.dot_general(a, b, (((ca,), (cb,)), ((), ())), preferred_element_type=F32)


def causal(x):
    rows = lax.broadcasted_iota(jnp.int32, x.shape, 0)
    cols = lax.broadcasted_iota(jnp.int32, x.shape, 1)
    return jnp.where(rows >= cols, x, 0.0).astype(BF)


def shape(dims, dtype):
    return jax.ShapeDtypeStruct(dims, dtype)


def prepare_kernel(core, *refs):
    for out, parts in ((refs[7], refs[:3]), (refs[8], refs[3:6])):
        for t in range(HEADS_CORE):
            for u in range(3):
                kind, head = place_of(t, u)
                out[t, :, u * HDIM : (u + 1) * HDIM] = parts[kind][:, cols(head)].astype(BF)
    refs[9][...] = refs[6][...]


def place_of(chunk, slot):
    place = 3 * (chunk % 2) + slot
    return place // 2, 2 * (chunk // 2) + place % 2


def cols(h):
    return slice(h * HDIM, (h + 1) * HDIM)


def prepare(core, master, cot):
    def spec(j, other):
        def index(i, c):
            return i, 2 * j + (1 - c[0] if other else c[0])

        return pl.BlockSpec((128, WIDTH), index)

    out = pl.BlockSpec((HEADS_CORE, 128, 3 * HDIM), lambda i, c: (0, i, 0))
    return pl.pallas_call(
        prepare_kernel,
        name="prepare",
        grid_spec=pltpu.PrefetchScalarGridSpec(
            num_scalar_prefetch=1,
            grid=(2,),
            in_specs=[spec(j, other) for other in (False, True) for j in range(3)]
            + [pl.BlockSpec((256, WIDTH), lambda i, c: (i, 1 - c[0]))],
            out_specs=(out, out, pl.BlockSpec((256, WIDTH), lambda i, c: (i, 0))),
        ),
        out_shape=(shape((HEADS_CORE, 256, 3 * HDIM), BF),) * 2 + (shape((BLOCK, WIDTH), BF),),
    )(core.reshape(1), *([master] * 6), cot)


def arrange_kernel(blocks, own, other, out):
    out[:BLOCK, :] = own[...]
    out[BLOCK:, :] = other[...]


def arrange(blocks, own, other):
    tile = pl.BlockSpec((BLOCK, 256), lambda i, b: (0, b[i]))
    return pl.pallas_call(
        arrange_kernel,
        name="arrange",
        grid_spec=pltpu.PrefetchScalarGridSpec(
            num_scalar_prefetch=1,
            grid=(8,),
            in_specs=[tile, tile],
            out_specs=pl.BlockSpec((ROWS, 256), lambda i, b: (0, i)),
        ),
        out_shape=shape((ROWS, own.shape[1]), BF),
    )(blocks, own, other)


def outer_kernel(k0, v0, k1, v1, kv):
    for pair, (keys, values) in enumerate(((k0, v0), (k1, v1))):
        for h in range(2):
            kv[2 * pair + h, 0] = dot(keys[:, cols(h)], values[:, cols(h)], 0, 0)


def own_states(first, second):
    keys = pl.BlockSpec((BLOCK, 256), lambda s: (s, 1))
    values = pl.BlockSpec((BLOCK, 256), lambda s: (s, 2))
    return pl.pallas_call(
        outer_kernel,
        name="outer",
        grid=(2,),
        in_specs=[keys, values, keys, values],
        out_specs=pl.BlockSpec((HEADS_CORE, 1, HDIM, HDIM), lambda s: (0, s, 0, 0)),
        out_shape=shape((HEADS_CORE, 2, HDIM, HDIM), F32),
    )(first, first, second, second)


def project(tokens, pieces):
    chunks = []
    for h, order in enumerate(GATHER_ORDERS):
        mine, low, high = pieces[3 * h : 3 * h + 3]
        theirs = (low, high)
        rows = []
        for i in range(8):
            flips = {"z0": i >> 2, "z1": (i >> 1) & 1}
            place = flips[order[0]] + 2 * flips[order[1]]
            rows.append(theirs[place // 2][place % 2] if i & 1 else mine[place])
        chunks.append(jnp.concatenate(rows, 0))
    weights = jnp.concatenate(chunks, 1)
    return jnp.dot(tokens, weights, preferred_element_type=F32).astype(BF)


def lower_scores(a, b):
    low = dot(a[256:], b, 1, 1)
    return causal(dot(a[:256], b[:256], 1, 1)), low[:, :256].astype(BF), causal(low[:, 256:])


def times(scores, x):
    first, left, right = scores
    low = jnp.concatenate([left, right], 1)
    return jnp.concatenate([dot(first, x[:256], 1, 0), dot(low, x, 1, 0)], 0)


def turned_times(scores, x):
    first, left, right = scores
    column = jnp.concatenate([first, left], 0)
    return jnp.concatenate([dot(column, x, 0, 0), dot(right, x[256:], 0, 0)], 0)


def running_kernel(received, out):
    total = jnp.zeros(received.shape[1:], F32)
    for place in range(received.shape[0]):
        out[place] = total.astype(BF)
        total = total + received[place]


def earlier_states(kv):
    cut = kv.reshape(16, -1, HDIM)
    received = lax.all_to_all(cut, ("x", "y"), 0, 0, tiled=True)
    sums = pl.pallas_call(
        running_kernel,
        name="running",
        out_shape=shape(received.shape, BF),
        in_specs=[VMEM],
        out_specs=VMEM,
    )(received)
    return lax.all_to_all(sums, ("x", "y"), 0, 0, tiled=True).reshape(kv.shape)


def head_of(ref, h, kind):
    return ref[:, pl.ds(pl.multiple_of((2 * "qkv".index(kind) + h) * HDIM, HDIM), HDIM)]


def head_cols(h):
    return pl.ds(pl.multiple_of(h * HDIM, HDIM), HDIM)


def each_head(body):
    def one(h, carry):
        body(h)
        return carry

    lax.fori_loop(0, 2, one, 0)


def pair_specs():
    qkv_rows = (BLOCK, 6 * HDIM)
    return [
        pl.BlockSpec(qkv_rows, lambda p, s, *_: (jnp.where(p == 0, s, 1), 0)),
        pl.BlockSpec(qkv_rows, lambda p, s, *_: (jnp.where(p == 0, 0, s), 0)),
    ]


def head_rows():
    return pl.BlockSpec((BLOCK, 256), lambda p, s, *_: (s, p))


def pick(first, second, h, kinds):
    pair = pl.program_id(0)
    return [jnp.where(pair == 0, head_of(first, h, j), head_of(second, h, j)) for j in kinds]


def within_kernel(first, second, out):
    @each_head
    def _(h):
        q, k, v = pick(first, second, h, "qkv")
        out[:, head_cols(h)] = times(lower_scores(q, k), v)


def local_scores(first, second):
    return pl.pallas_call(
        within_kernel,
        name="within",
        grid=(2, 2),
        in_specs=pair_specs(),
        out_specs=head_rows(),
        out_shape=shape((ROWS, WIDTH), F32),
    )(first, second)


def forward_kernel(core, first, second, within, state, cot_own, cot_other, attended, grad, qg):
    s = pl.program_id(1)

    @each_head
    def _(h):
        (q,) = pick(first, second, h, "q")
        at = head_cols(h)
        mixed = within[:, at] + dot(q, state[h, 0], 1, 0)
        inverse = lax.rsqrt(jnp.mean(mixed * mixed, -1, keepdims=True) + EPS_NORM)
        normed = mixed * inverse
        attended[:, at] = normed.astype(BF)
        out_grad = jnp.where(s == 0, cot_own[:, at], cot_other[:, at]).astype(F32)
        along = jnp.mean(out_grad * normed, -1, keepdims=True)
        g = (inverse * (out_grad - normed * along)).astype(BF)
        grad[:, at] = g
        qg[h, 0] = dot(q, g, 0, 0).astype(BF)


def forward(core, first, second, within, state, cot_own, cot_other):
    rows = head_rows()
    states = pl.BlockSpec((2, 1, HDIM, HDIM), lambda p, s, c: (p, s, 0, 0))
    queries = (BLOCK, 2 * HDIM)
    return pl.pallas_call(
        forward_kernel,
        name="forward",
        grid_spec=pltpu.PrefetchScalarGridSpec(
            num_scalar_prefetch=1,
            grid=(2, 2),
            in_specs=[
                pl.BlockSpec(queries, lambda p, s, c: (jnp.where(p == 0, s, 1), 0)),
                pl.BlockSpec(queries, lambda p, s, c: (jnp.where(p == 0, 0, s), 0)),
                rows,
                states,
                pl.BlockSpec((BLOCK, 256), lambda p, s, c: (0, 2 * c[0] + p)),
                pl.BlockSpec((BLOCK, 256), lambda p, s, c: (0, p)),
            ],
            out_specs=(rows, rows, states),
        ),
        out_shape=(
            shape((ROWS, WIDTH), BF),
            shape((ROWS, WIDTH), BF),
            shape((HEADS_CORE, 2, HDIM, HDIM), BF),
        ),
    )(core.reshape(1), first, second, within, state, cot_own, cot_other)


def backward_kernel(pair, qkv, grad, state, dq, dkv):
    for h in range(2):
        q, k, v = [qkv[:, cols(2 * j + h)] for j in range(3)]
        at = cols(h)
        g = grad[:, at]
        back = lower_scores(g, v)
        dq[:, at] = (times(back, k) + dot(g, state[h, 0], 1, 1)).astype(BF)
        dkv[0, :, at] = turned_times(back, q)
        dkv[1, :, at] = turned_times(lower_scores(q, k), g)


def backward(pair, qkv, grad, state):
    return pl.pallas_call(
        backward_kernel,
        name="backward",
        grid_spec=pltpu.PrefetchScalarGridSpec(
            num_scalar_prefetch=1,
            grid=(2,),
            in_specs=[
                pl.BlockSpec((BLOCK, 6 * HDIM), lambda s, p: (s, 0)),
                pl.BlockSpec((BLOCK, 256), lambda s, p: (s, p[0])),
                pl.BlockSpec((2, 1, HDIM, HDIM), lambda s, p: (p[0], s, 0, 0)),
            ],
            out_specs=(
                pl.BlockSpec((BLOCK, 256), lambda s, p: (s, 0)),
                pl.BlockSpec((2, BLOCK, 256), lambda s, p: (0, s, 0)),
            ),
        ),
        out_shape=(shape((ROWS, 256), BF), shape((2, ROWS, 256), F32)),
    )(jnp.full((1,), pair, jnp.int32), qkv, grad, state)


def multiply_blocks(turned, tokens, out):
    def blocks(i, carry):
        at = pl.ds(pl.multiple_of(i * 512, 512), 512)
        piece = dot(turned[...], tokens[:, at], 1, 0).astype(BF)
        for half in range(2):
            for j in range(2):
                out[half, 2 * i + j] = piece[half * 256 : (half + 1) * 256, j * 256 : (j + 1) * 256]
        return carry

    lax.fori_loop(0, tokens.shape[1] // 512, blocks, 0)


def query_gradient_kernel(q0, q1, tokens, out, turned):
    turned[:256, :] = q0[...].T
    turned[256:, :] = q1[...].T
    multiply_blocks(turned, tokens, out)


def gradient_kernel(kind, first, second, d_first, d_second, state, tokens, out, turned):
    for pair, (rows, within) in enumerate(((first, d_first), (second, d_second))):
        for h in range(2):
            head = 2 * pair + h
            for s in range(2):
                span = slice(s * BLOCK, (s + 1) * BLOCK)
                later = dot(rows[span, cols(h)], state[head, s], 1, 1 - kind)
                total = within[0, span, cols(h)] + later
                turned[cols(head), span] = total.astype(BF).T

    multiply_blocks(turned, tokens, out)


def gradient_call(kernel, ins, specs, tokens):
    blocks = tokens.shape[1] // 256
    return pl.pallas_call(
        kernel,
        grid=(1,),
        in_specs=specs + [VMEM],
        out_specs=VMEM,
        out_shape=shape((2, blocks, 256, 256), BF),
        scratch_shapes=[pltpu.VMEM((WIDTH, ROWS), BF)],
    )(*ins, tokens)


def query_gradient(q0, q1, tokens):
    return gradient_call(query_gradient_kernel, (q0, q1), [VMEM] * 2, tokens)


def key_value_gradient(kind, first, second, d_first, d_second, state, tokens):
    rows = pl.BlockSpec((ROWS, 256), lambda _: (0, 2 - kind))
    within = pl.BlockSpec((1, ROWS, 256), lambda _: (kind, 0, 0))
    specs = [rows, rows, within, within, VMEM]
    ins = (first, second, d_first, d_second, state)
    kernel = functools.partial(gradient_kernel, kind)
    return gradient_call(kernel, ins, specs, tokens)


def parts_of(partial):
    return [partial[i].reshape(2, 2, 2, 256, 256) for i in range(2)]


def wide(x):
    return x.astype(F32)


def add(a, b):
    return (wide(a) + wide(b)).astype(BF)


def reduce_steps(part, order):
    left = ["z0", "z1", "flat"]
    for dim in order:
        name = dim if dim[0] == "z" else "flat"
        axis = left.index(name)
        left.remove(name)
        if name == "flat":
            keeps = colour() ^ place_bit(dim)
            send = lax.dynamic_index_in_dim(part, 1 - keeps, axis, False)
            keep = lax.dynamic_index_in_dim(part, keeps, axis, False)
        else:
            send = lax.index_in_dim(part, 1, axis, False)
            keep = lax.index_in_dim(part, 0, axis, False)
        received = yield swap(send, dim)
        part = add(keep, received)
    yield part


def finish_group(parts, exchanged, last):
    total = jnp.stack(parts)
    for dim in exchanged:
        total = add(total, swap(total, dim))
    return total, swap(total, last)


def later_steps(total, later):
    total = wide(total)
    carried = jnp.zeros_like(total)
    for dim in ("y0", "y1", "x0", "x1"):
        received = yield swap(total.astype(BF), dim)
        received = wide(received)
        upper = (lax.axis_index(dim[0]) >> int(dim[1])) & 1
        carried = carried + jnp.where(upper == (0 if later else 1), received, 0.0)
        total = total + received
    yield carried.astype(BF)


def sort_kernel(holds, *refs):
    kept, sent = refs[-2:]
    for g, (members, _, _) in enumerate(GROUPS):
        straight = holds[g] == 1
        for j, p in enumerate(members):
            at = slice(p * 256, (p + 1) * 256)
            here, there = refs[2 * g][j].T, refs[2 * g + 1][j].T
            kept[:, at] = jnp.where(straight, here, there)
            sent[:, at] = jnp.where(straight, there, here)


def sort_pieces(holds, finished):
    return pl.pallas_call(
        sort_kernel,
        name="sort_pieces",
        in_specs=[pl.BlockSpec(memory_space=pltpu.SMEM)] + [VMEM] * len(finished),
        out_specs=(VMEM, VMEM),
        out_shape=(shape((256, 3 * WIDTH), BF),) * 2,
    )(holds, *finished)


def adam_kernel(core, kept, received, weights, first, second, out_weights, out_first, out_second):
    for block in range(6):
        at = slice(block * WIDTH, (block + 1) * WIDTH)
        source = slice((block // 2) * WIDTH, (block // 2 + 1) * WIDTH)
        gradient = jnp.where(block % 2 == core[0], kept[:, source], received[:, source]).astype(F32)
        new_first = BETA_ONE * first[:, at] + (1.0 - BETA_ONE) * gradient
        new_second = BETA_TWO * second[:, at] + (1.0 - BETA_TWO) * gradient * gradient
        first_hat = new_first / (1.0 - BETA_ONE**STEP)
        second_hat = new_second / (1.0 - BETA_TWO**STEP)
        out_first[:, at] = new_first
        out_second[:, at] = new_second
        out_weights[:, at] = weights[:, at] - LEARN_RATE * (
            first_hat / (jnp.sqrt(second_hat) + EPS_ADAM) + DECAY_WEIGHT * weights[:, at]
        )


def adam(core, kept, received, *arrays):
    piece = pl.BlockSpec((32, 3 * WIDTH), lambda i, c: (i, 0))
    block = pl.BlockSpec((32, 6 * WIDTH), lambda i, c: (i, 0))
    return pl.pallas_call(
        adam_kernel,
        name="adam",
        grid_spec=pltpu.PrefetchScalarGridSpec(
            num_scalar_prefetch=1,
            grid=(8,),
            in_specs=[piece, piece, block, block, block],
            out_specs=(block,) * 3,
        ),
        out_shape=tuple(shape(x.shape, F32) for x in arrays),
    )(core.reshape(1), kept, received, *arrays)


def gather_step(step, mine):
    got = []
    for h in range(2):
        got.append(swap(mine[h], GATHER_ORDERS[h][step]))
    return [jnp.concatenate([mine[h], got[h]], 0) for h in range(2)]


def exchange_colours(mine):
    pieces = []
    for h, axis in enumerate("xy"):
        pieces.append(mine[h])
        for side in range(2):
            pieces.append(swap(mine[h][2 * side : 2 * side + 2], f"{axis}{side}"))
    return pieces


def step(tokens, weights_master, adam_first, adam_second, cotangent):
    core = lax.axis_index("c")
    own = tokens[0]
    straight = colour() == core

    held, outgoing, cot_out = prepare(core, weights_master, cotangent[0])
    traded = swap(outgoing, "c")
    other = swap(own, "c")
    cot_other = swap(cot_out, "c")

    blocks = block_order()
    mine = jnp.where(straight, held, traded)
    first = gather_step(0, [mine[0][None], mine[1][None]])
    first = gather_step(1, first)
    both = arrange(blocks, own, other)
    first, mine, both = barrier((first, mine, both))
    pieces = exchange_colours(first)
    second = gather_step(0, [mine[2][None], mine[3][None]])
    second = gather_step(1, second)
    qkv_first = project(both, pieces)
    second, qkv_first = barrier((second, qkv_first))
    qkv_second = project(both, exchange_colours(second))

    state = earlier_states(own_states(qkv_first, qkv_second))
    within = local_scores(qkv_first, qkv_second)
    attended, grad, qg = forward(
        core, qkv_first, qkv_second, within, state, cotangent[0], cot_other
    )

    steps = later_steps(qg, True)
    received = next(steps)
    q0, d0 = backward(0, qkv_first, grad, state)
    received, q0, d0, grad = barrier((received, q0, d0, grad))
    received = steps.send(received)
    q1, d1 = backward(1, qkv_second, grad, state)
    received, q0, q1, d1 = barrier((received, q0, q1, d1))
    received = steps.send(received)
    parts = parts_of(query_gradient(q0, q1, both))
    received, parts = barrier((received, parts))
    received = steps.send(received)
    queries = [reduce_steps(part, order) for part, order in zip(parts, HALVING)]
    arrived = [next(part) for part in queries]
    later = steps.send(received)

    operands = (qkv_first, qkv_second, d0, d1, later, both)
    parts = parts_of(key_value_gradient(0, *operands))
    parts, arrived, operands = barrier((parts, arrived, operands))
    arrived = [part.send(x) for part, x in zip(queries, arrived)]
    others = [reduce_steps(part, order) for part, order in zip(parts, HALVING[2:])]
    moving = [next(part) for part in others]
    parts = parts_of(key_value_gradient(1, *operands))
    parts, arrived = barrier((parts, arrived))
    arrived = [part.send(x) for part, x in zip(queries, arrived)]
    others += [reduce_steps(part, order) for part, order in zip(parts, HALVING[4:])]
    moving += [next(part) for part in others[2:]]
    reduced = [part.send(x) for part, x in zip(queries, arrived)]
    for _ in range(3):
        moving = [part.send(x) for part, x in zip(others, moving)]
    reduced += moving

    attended_other = swap(attended[BLOCK:], "c")
    low = jnp.where(core == 0, attended[:BLOCK], attended_other)
    high = jnp.where(core == 0, attended_other, attended[:BLOCK])
    attended_out = jnp.concatenate([low, high], 1)[None]

    holds, finished = [], []
    for members, exchanged, last in GROUPS:
        holds.append(place_bit(last) == core)
        finished += finish_group([reduced[p] for p in members], exchanged, last)
    kept, sent = sort_pieces(jnp.stack(holds).astype(jnp.int32), finished)
    received = swap(sent, "c")
    new_weights, new_first, new_second = adam(
        core, kept, received, weights_master, adam_first, adam_second
    )
    return (attended_out, new_weights, new_first, new_second)


def solution(mesh):
    torus = Mesh(mesh.devices.reshape(4, 4, 4, 2), ("x", "y", "z", "c"))
    rows = P(("z", "c"), ("x", "y"), None)
    shard = P(("z", "c"), None)
    return jax.shard_map(
        step,
        mesh=torus,
        in_specs=(rows, shard, shard, shard, rows),
        out_specs=(rows, shard, shard, shard),
        check_vma=False,
    )
```

```python
import jax
import jax.numpy as jnp
from jax import lax
from jax.experimental import pallas as pl
from jax.experimental.pallas import tpu as pltpu
from jax.sharding import Mesh, PartitionSpec as P


HDIM = 128
BLOCK = 512
STEP = 100
HEADS_CORE = 4

EPS_NORM = 1e-05
BETA_ONE = 0.9
BETA_TWO = 0.95
LEARN_RATE = 0.001
DECAY_WEIGHT = 0.1
EPS_ADAM = 1e-08

BF = jnp.bfloat16
F32 = jnp.float32


PAIRS = {
    "0": [(0, 1), (1, 0), (2, 3), (3, 2)],
    "1": [(1, 2), (2, 1), (3, 0), (0, 3)],
}
CORE_SWAP = [(0, 1), (1, 0)]

GATHER_ORDERS = [("z0", "z1"), ("z1", "z0")]
HALVING = [
    ("x0", "z0", "z1"),
    ("y0", "z1", "z0"),
    ("x0", "z0", "z1"),
    ("y0", "z1", "z0"),
    ("x1", "z0", "z1"),
    ("y1", "z1", "z0"),
]
GROUPS = [
    ((0, 2), ("x1", "y1", "y0"), "x0"),
    ((1, 3), ("y1", "x1", "x0"), "y0"),
    ((4,), ("y0", "x0", "y1"), "x1"),
    ((5,), ("x0", "y0", "x1"), "y1"),
]
WIDTH = HEADS_CORE * HDIM
ROWS = 2 * BLOCK
VMEM = pl.BlockSpec(memory_space=pltpu.VMEM)
barrier = lax.optimization_barrier


def swap(x, dim):
    if dim == "c":
        return lax.ppermute(x, "c", CORE_SWAP)
    return lax.ppermute(x, dim[0], PAIRS[dim[1]])


def gray(place):
    return place ^ (place >> 1)


def place_bit(dim):
    code = gray(lax.axis_index(dim[0]))
    return (code >> int(dim[1])) & 1


def colour():
    return (lax.axis_index("x") + lax.axis_index("y")) & 1


def block_order():
    blocks = []
    for i in range(8):
        code = gray(lax.axis_index("z")) ^ (i >> 2) ^ (((i >> 1) & 1) << 1)
        blocks.append(2 * (code ^ (code >> 1)) + (colour() ^ (i & 1)))
    return jnp.stack(blocks).astype(jnp.int32)


def dot(a, b, ca, cb):
    return lax.dot_general(a, b, (((ca,), (cb,)), ((), ())), preferred_element_type=F32)


def causal(x):
    rows = lax.broadcasted_iota(jnp.int32, x.shape, 0)
    cols = lax.broadcasted_iota(jnp.int32, x.shape, 1)
    return jnp.where(rows >= cols, x, 0.0).astype(BF)


def shape(dims, dtype):
    return jax.ShapeDtypeStruct(dims, dtype)


def prepare_kernel(core, *refs):
    for out, parts in ((refs[7], refs[:3]), (refs[8], refs[3:6])):
        for t in range(HEADS_CORE):
            for u in range(3):
                kind, head = place_of(t, u)
                out[t, :, u * HDIM : (u + 1) * HDIM] = parts[kind][:, cols(head)].astype(BF)
    refs[9][...] = refs[6][...]


def place_of(chunk, slot):
    place = 3 * (chunk % 2) + slot
    return place // 2, 2 * (chunk // 2) + place % 2


def cols(h):
    return slice(h * HDIM, (h + 1) * HDIM)


def prepare(core, master, cot):
    def spec(j, other):
        def index(i, c):
            return i, 2 * j + (1 - c[0] if other else c[0])

        return pl.BlockSpec((128, WIDTH), index)

    out = pl.BlockSpec((HEADS_CORE, 128, 3 * HDIM), lambda i, c: (0, i, 0))
    return pl.pallas_call(
        prepare_kernel,
        name="prepare",
        grid_spec=pltpu.PrefetchScalarGridSpec(
            num_scalar_prefetch=1,
            grid=(2,),
            in_specs=[spec(j, other) for other in (False, True) for j in range(3)]
            + [pl.BlockSpec((256, WIDTH), lambda i, c: (i, 1 - c[0]))],
            out_specs=(out, out, pl.BlockSpec((256, WIDTH), lambda i, c: (i, 0))),
        ),
        out_shape=(shape((HEADS_CORE, 256, 3 * HDIM), BF),) * 2 + (shape((BLOCK, WIDTH), BF),),
    )(core.reshape(1), *([master] * 6), cot)


def arrange_kernel(blocks, own, other, out):
    out[:BLOCK, :] = own[...]
    out[BLOCK:, :] = other[...]


def arrange(blocks, own, other):
    tile = pl.BlockSpec((BLOCK, 256), lambda i, b: (0, b[i]))
    return pl.pallas_call(
        arrange_kernel,
        name="arrange",
        grid_spec=pltpu.PrefetchScalarGridSpec(
            num_scalar_prefetch=1,
            grid=(8,),
            in_specs=[tile, tile],
            out_specs=pl.BlockSpec((ROWS, 256), lambda i, b: (0, i)),
        ),
        out_shape=shape((ROWS, own.shape[1]), BF),
    )(blocks, own, other)


def outer_kernel(k0, v0, k1, v1, kv):
    for pair, (keys, values) in enumerate(((k0, v0), (k1, v1))):
        for h in range(2):
            kv[2 * pair + h, 0] = dot(keys[:, cols(h)], values[:, cols(h)], 0, 0)


def own_states(first, second):
    keys = pl.BlockSpec((BLOCK, 256), lambda s: (s, 1))
    values = pl.BlockSpec((BLOCK, 256), lambda s: (s, 2))
    return pl.pallas_call(
        outer_kernel,
        name="outer",
        grid=(2,),
        in_specs=[keys, values, keys, values],
        out_specs=pl.BlockSpec((HEADS_CORE, 1, HDIM, HDIM), lambda s: (0, s, 0, 0)),
        out_shape=shape((HEADS_CORE, 2, HDIM, HDIM), F32),
    )(first, first, second, second)


def project(tokens, pieces):
    chunks = []
    for h, order in enumerate(GATHER_ORDERS):
        mine, low, high = pieces[3 * h : 3 * h + 3]
        theirs = (low, high)
        rows = []
        for i in range(8):
            flips = {"z0": i >> 2, "z1": (i >> 1) & 1}
            place = flips[order[0]] + 2 * flips[order[1]]
            rows.append(theirs[place // 2][place % 2] if i & 1 else mine[place])
        chunks.append(jnp.concatenate(rows, 0))
    weights = jnp.concatenate(chunks, 1)
    return jnp.dot(tokens, weights, preferred_element_type=F32).astype(BF)


def lower_scores(a, b):
    low = dot(a[256:], b, 1, 1)
    return causal(dot(a[:256], b[:256], 1, 1)), low[:, :256].astype(BF), causal(low[:, 256:])


def times(scores, x):
    first, left, right = scores
    low = jnp.concatenate([left, right], 1)
    return jnp.concatenate([dot(first, x[:256], 1, 0), dot(low, x, 1, 0)], 0)


def turned_times(scores, x):
    first, left, right = scores
    column = jnp.concatenate([first, left], 0)
    return jnp.concatenate([dot(column, x, 0, 0), dot(right, x[256:], 0, 0)], 0)


def running_kernel(received, out):
    total = jnp.zeros(received.shape[1:], F32)
    for place in range(received.shape[0]):
        out[place] = total.astype(BF)
        total = total + received[place]


def earlier_states(kv):
    cut = kv.reshape(16, -1, HDIM)
    received = lax.all_to_all(cut, ("x", "y"), 0, 0, tiled=True)
    sums = pl.pallas_call(
        running_kernel,
        name="running",
        out_shape=shape(received.shape, BF),
        in_specs=[VMEM],
        out_specs=VMEM,
    )(received)
    return lax.all_to_all(sums, ("x", "y"), 0, 0, tiled=True).reshape(kv.shape)


def head_of(ref, h, kind):
    return ref[:, pl.ds(pl.multiple_of((2 * "qkv".index(kind) + h) * HDIM, HDIM), HDIM)]


def head_cols(h):
    return pl.ds(pl.multiple_of(h * HDIM, HDIM), HDIM)


def each_head(body):
    def one(h, carry):
        body(h)
        return carry

    lax.fori_loop(0, 2, one, 0)


def pair_specs():
    qkv_rows = (BLOCK, 6 * HDIM)
    return [
        pl.BlockSpec(qkv_rows, lambda p, s, *_: (jnp.where(p == 0, s, 1), 0)),
        pl.BlockSpec(qkv_rows, lambda p, s, *_: (jnp.where(p == 0, 0, s), 0)),
    ]


def head_rows():
    return pl.BlockSpec((BLOCK, 256), lambda p, s, *_: (s, p))


def pick(first, second, h, kinds):
    pair = pl.program_id(0)
    return [jnp.where(pair == 0, head_of(first, h, j), head_of(second, h, j)) for j in kinds]


def within_kernel(first, second, out):
    @each_head
    def _(h):
        q, k, v = pick(first, second, h, "qkv")
        out[:, head_cols(h)] = times(lower_scores(q, k), v)


def local_scores(first, second):
    return pl.pallas_call(
        within_kernel,
        name="within",
        grid=(2, 2),
        in_specs=pair_specs(),
        out_specs=head_rows(),
        out_shape=shape((ROWS, WIDTH), F32),
    )(first, second)


def forward_kernel(core, first, second, within, state, cot_own, cot_other, attended, grad, qg):
    s = pl.program_id(1)

    @each_head
    def _(h):
        (q,) = pick(first, second, h, "q")
        at = head_cols(h)
        mixed = within[:, at] + dot(q, state[h, 0], 1, 0)
        inverse = lax.rsqrt(jnp.mean(mixed * mixed, -1, keepdims=True) + EPS_NORM)
        normed = mixed * inverse
        attended[:, at] = normed.astype(BF)
        out_grad = jnp.where(s == 0, cot_own[:, at], cot_other[:, at]).astype(F32)
        along = jnp.mean(out_grad * normed, -1, keepdims=True)
        g = (inverse * (out_grad - normed * along)).astype(BF)
        grad[:, at] = g
        qg[h, 0] = dot(q, g, 0, 0).astype(BF)


def forward(core, first, second, within, state, cot_own, cot_other):
    rows = head_rows()
    states = pl.BlockSpec((2, 1, HDIM, HDIM), lambda p, s, c: (p, s, 0, 0))
    queries = (BLOCK, 2 * HDIM)
    return pl.pallas_call(
        forward_kernel,
        name="forward",
        grid_spec=pltpu.PrefetchScalarGridSpec(
            num_scalar_prefetch=1,
            grid=(2, 2),
            in_specs=[
                pl.BlockSpec(queries, lambda p, s, c: (jnp.where(p == 0, s, 1), 0)),
                pl.BlockSpec(queries, lambda p, s, c: (jnp.where(p == 0, 0, s), 0)),
                rows,
                states,
                pl.BlockSpec((BLOCK, 256), lambda p, s, c: (0, 2 * c[0] + p)),
                pl.BlockSpec((BLOCK, 256), lambda p, s, c: (0, p)),
            ],
            out_specs=(rows, rows, states),
        ),
        out_shape=(
            shape((ROWS, WIDTH), BF),
            shape((ROWS, WIDTH), BF),
            shape((HEADS_CORE, 2, HDIM, HDIM), BF),
        ),
    )(core.reshape(1), first, second, within, state, cot_own, cot_other)


def backward_kernel(pair, qkv, grad, state, dq, dkv):
    for h in range(2):
        q, k, v = [qkv[:, cols(2 * j + h)] for j in range(3)]
        at = cols(h)
        g = grad[:, at]
        back = lower_scores(g, v)
        dq[:, at] = (times(back, k) + dot(g, state[h, 0], 1, 1)).astype(BF)
        dkv[0, :, at] = turned_times(back, q)
        dkv[1, :, at] = turned_times(lower_scores(q, k), g)


def backward(pair, qkv, grad, state):
    return pl.pallas_call(
        backward_kernel,
        name="backward",
        grid_spec=pltpu.PrefetchScalarGridSpec(
            num_scalar_prefetch=1,
            grid=(2,),
            in_specs=[
                pl.BlockSpec((BLOCK, 6 * HDIM), lambda s, p: (s, 0)),
                pl.BlockSpec((BLOCK, 256), lambda s, p: (s, p[0])),
                pl.BlockSpec((2, 1, HDIM, HDIM), lambda s, p: (p[0], s, 0, 0)),
            ],
            out_specs=(
                pl.BlockSpec((BLOCK, 256), lambda s, p: (s, 0)),
                pl.BlockSpec((2, BLOCK, 256), lambda s, p: (0, s, 0)),
            ),
        ),
        out_shape=(shape((ROWS, 256), BF), shape((2, ROWS, 256), F32)),
    )(jnp.full((1,), pair, jnp.int32), qkv, grad, state)


def multiply_blocks(keeps, turned, tokens, outs):
    def blocks(i, carry):
        at = pl.ds(pl.multiple_of(i * 512, 512), 512)
        piece = dot(turned[...], tokens[:, at], 1, 0).astype(BF)
        for part in range(2):
            sent, kept = outs[2 * part], outs[2 * part + 1]
            first = piece[part * 256 : (part + 1) * 256, :256]
            second = piece[part * 256 : (part + 1) * 256, 256:]
            kept[i] = jnp.where(keeps[part] == 0, first, second)
            sent[i] = jnp.where(keeps[part] == 0, second, first)
        return carry

    lax.fori_loop(0, tokens.shape[1] // 512, blocks, 0)


def query_gradient_kernel(keeps, q0, q1, tokens, s0, k0, s1, k1, turned):
    turned[:256, :] = q0[...].T
    turned[256:, :] = q1[...].T
    multiply_blocks(keeps, turned, tokens, (s0, k0, s1, k1))


def gradient_kernel(keeps, first, second, d_first, d_second, state, tokens, *refs):
    turned = refs[-1]
    for kind in range(2):
        sides = ((first, d_first), (second, d_second))
        for pair, (qkv, within) in enumerate(sides):

            @each_head
            def _(h):
                head = 2 * pair + h
                at = head_cols(h)
                for s in range(2):
                    span = slice(s * BLOCK, (s + 1) * BLOCK)
                    source = qkv[span, head_cols(4 - 2 * kind + h)]
                    later = dot(source, state[head, s], 1, 1 - kind)
                    total = within[kind, span, at] + later
                    turned[head_cols(head), span] = total.astype(BF).T

        multiply_blocks(keeps.at[pl.ds(2 * kind, 2)], turned, tokens, refs[4 * kind : 4 * kind + 4])


def gradient_call(kernel, first, ins, specs, tokens):
    count = len(first)
    keeps = jnp.stack([colour() ^ place_bit(HALVING[p][0]) for p in first]).astype(jnp.int32)
    return pl.pallas_call(
        kernel,
        in_specs=[pl.BlockSpec(memory_space=pltpu.SMEM)] + specs + [VMEM],
        out_specs=(VMEM,) * (2 * count),
        out_shape=(shape((4, 256, 256), BF),) * (2 * count),
        scratch_shapes=[pltpu.VMEM((WIDTH, ROWS), BF)],
    )(keeps, *ins, tokens)


def query_gradient(q0, q1, tokens):
    return gradient_call(query_gradient_kernel, (0, 1), (q0, q1), [VMEM] * 2, tokens)


def key_value_gradient(first, second, d_first, d_second, state, tokens):
    ins = (first, second, d_first, d_second, state)
    return gradient_call(gradient_kernel, (2, 3, 4, 5), ins, [VMEM] * 5, tokens)


def wide(x):
    return x.astype(F32)


def add(a, b):
    return (wide(a) + wide(b)).astype(BF)


def reduce_part(sent, kept, order):
    part = add(kept, swap(sent, order[0])).reshape(2, 2, 256, 256)
    for i, dim in enumerate(order[1:]):
        axis = int(dim[1]) if i == 0 else 0
        send = lax.index_in_dim(part, 1, axis, False)
        part = add(lax.index_in_dim(part, 0, axis, False), swap(send, dim))
    return part


def finish_group(parts, exchanged, last):
    total = jnp.stack(parts)
    for dim in exchanged:
        total = add(total, swap(total, dim))
    return total, swap(total, last)


def later_steps(total, later):
    total = wide(total)
    carried = jnp.zeros_like(total)
    for dim in ("y0", "y1", "x0", "x1"):
        received = yield swap(total.astype(BF), dim)
        received = wide(received)
        upper = (lax.axis_index(dim[0]) >> int(dim[1])) & 1
        carried = carried + jnp.where(upper == (0 if later else 1), received, 0.0)
        total = total + received
    yield carried.astype(BF)


def sort_kernel(holds, *refs):
    kept, sent = refs[-2:]
    for g, (members, _, _) in enumerate(GROUPS):
        straight = holds[g] == 1
        for j, p in enumerate(members):
            at = slice(p * 256, (p + 1) * 256)
            here, there = refs[2 * g][j].T, refs[2 * g + 1][j].T
            kept[:, at] = jnp.where(straight, here, there)
            sent[:, at] = jnp.where(straight, there, here)


def sort_pieces(holds, finished):
    return pl.pallas_call(
        sort_kernel,
        name="sort_pieces",
        in_specs=[pl.BlockSpec(memory_space=pltpu.SMEM)] + [VMEM] * len(finished),
        out_specs=(VMEM, VMEM),
        out_shape=(shape((256, 3 * WIDTH), BF),) * 2,
    )(holds, *finished)


def join_kernel(core, own, other, out):
    straight = core[0] == 0
    out[0, :, :WIDTH] = jnp.where(straight, own[...], other[...])
    out[0, :, WIDTH:] = jnp.where(straight, other[...], own[...])


def join_heads(core, own, other):
    half = pl.BlockSpec((256, WIDTH), lambda i, c: (i, 0))
    return pl.pallas_call(
        join_kernel,
        name="join_heads",
        grid_spec=pltpu.PrefetchScalarGridSpec(
            num_scalar_prefetch=1,
            grid=(2,),
            in_specs=[half, half],
            out_specs=pl.BlockSpec((1, 256, 2 * WIDTH), lambda i, c: (0, i, 0)),
        ),
        out_shape=shape((1, BLOCK, 2 * WIDTH), BF),
    )(core.reshape(1), own, other)


def adam_kernel(core, kept, received, weights, first, second, out_weights, out_first, out_second):
    for block in range(6):
        at = slice(block * WIDTH, (block + 1) * WIDTH)
        source = slice((block // 2) * WIDTH, (block // 2 + 1) * WIDTH)
        gradient = jnp.where(block % 2 == core[0], kept[:, source], received[:, source]).astype(F32)
        new_first = BETA_ONE * first[:, at] + (1.0 - BETA_ONE) * gradient
        new_second = BETA_TWO * second[:, at] + (1.0 - BETA_TWO) * gradient * gradient
        first_hat = new_first * (1.0 / (1.0 - BETA_ONE**STEP))
        second_hat = new_second * (1.0 / (1.0 - BETA_TWO**STEP))
        out_first[:, at] = new_first
        out_second[:, at] = new_second
        out_weights[:, at] = weights[:, at] - LEARN_RATE * (
            first_hat / (jnp.sqrt(second_hat) + EPS_ADAM) + DECAY_WEIGHT * weights[:, at]
        )


def adam(core, kept, received, *arrays):
    piece = pl.BlockSpec((32, 3 * WIDTH), lambda i, c: (i, 0))
    block = pl.BlockSpec((32, 6 * WIDTH), lambda i, c: (i, 0))
    return pl.pallas_call(
        adam_kernel,
        name="adam",
        grid_spec=pltpu.PrefetchScalarGridSpec(
            num_scalar_prefetch=1,
            grid=(8,),
            in_specs=[piece, piece, block, block, block],
            out_specs=(block,) * 3,
        ),
        out_shape=tuple(shape(x.shape, F32) for x in arrays),
    )(core.reshape(1), kept, received, *arrays)


def gather_step(step, mine):
    got = []
    for h in range(2):
        got.append(swap(mine[h], GATHER_ORDERS[h][step]))
    return [jnp.concatenate([mine[h], got[h]], 0) for h in range(2)]


def exchange_colours(mine):
    pieces = []
    for h, axis in enumerate("xy"):
        pieces.append(mine[h])
        for side in range(2):
            pieces.append(swap(mine[h][2 * side : 2 * side + 2], f"{axis}{side}"))
    return pieces


def step(tokens, weights_master, adam_first, adam_second, cotangent):
    core = lax.axis_index("c")
    own = tokens[0]
    straight = colour() == core

    held, outgoing, cot_out = prepare(core, weights_master, cotangent[0])
    traded = swap(outgoing, "c")
    other = swap(own, "c")
    cot_other = swap(cot_out, "c")

    blocks = block_order()
    mine = jnp.where(straight, held, traded)
    first = gather_step(0, [mine[0][None], mine[1][None]])
    first = gather_step(1, first)
    both = arrange(blocks, own, other)
    first, mine, both = barrier((first, mine, both))
    pieces = exchange_colours(first)
    second = gather_step(0, [mine[2][None], mine[3][None]])
    second = gather_step(1, second)
    qkv_first = project(both, pieces)
    second, qkv_first = barrier((second, qkv_first))
    qkv_second = project(both, exchange_colours(second))

    state = earlier_states(own_states(qkv_first, qkv_second))
    within = local_scores(qkv_first, qkv_second)
    attended, grad, qg = forward(
        core, qkv_first, qkv_second, within, state, cotangent[0], cot_other
    )

    steps = later_steps(qg, True)
    received = next(steps)
    q0, d0 = backward(0, qkv_first, grad, state)
    received, q0, d0, grad = barrier((received, q0, d0, grad))
    received = steps.send(received)
    q1, d1 = backward(1, qkv_second, grad, state)
    received, q0, q1, d1 = barrier((received, q0, q1, d1))
    received = steps.send(received)
    parts = query_gradient(q0, q1, both)
    received, parts = barrier((received, parts))
    received = steps.send(received)
    later = steps.send(received)
    parts += key_value_gradient(qkv_first, qkv_second, d0, d1, later, both)
    reduced = [
        reduce_part(parts[2 * p], parts[2 * p + 1], order) for p, order in enumerate(HALVING)
    ]

    attended_other = swap(attended[BLOCK:], "c")
    attended_out = join_heads(core, attended, attended_other)

    holds, finished = [], []
    for members, exchanged, last in GROUPS:
        holds.append(place_bit(last) == core)
        finished += finish_group([reduced[p] for p in members], exchanged, last)
    kept, sent = sort_pieces(jnp.stack(holds).astype(jnp.int32), finished)
    received = swap(sent, "c")
    new_weights, new_first, new_second = adam(
        core, kept, received, weights_master, adam_first, adam_second
    )
    return (attended_out, new_weights, new_first, new_second)


def solution(mesh):
    torus = Mesh(mesh.devices.reshape(4, 4, 4, 2), ("x", "y", "z", "c"))
    rows = P(("z", "c"), ("x", "y"), None)
    shard = P(("z", "c"), None)
    return jax.shard_map(
        step,
        mesh=torus,
        in_specs=(rows, shard, shard, shard, rows),
        out_specs=(rows, shard, shard, shard),
        check_vma=False,
    )
```

```python
import jax
import jax.numpy as jnp
from jax import lax
from jax.experimental import pallas as pl
from jax.experimental.pallas import tpu as pltpu
from jax.sharding import Mesh, PartitionSpec as P


HDIM = 128
BLOCK = 512
STEP = 100
HEADS_CORE = 4

EPS_NORM = 1e-05
BETA_ONE = 0.9
BETA_TWO = 0.95
LEARN_RATE = 0.001
DECAY_WEIGHT = 0.1
EPS_ADAM = 1e-08

BF = jnp.bfloat16
F32 = jnp.float32


PAIRS = {
    "0": [(0, 1), (1, 0), (2, 3), (3, 2)],
    "1": [(1, 2), (2, 1), (3, 0), (0, 3)],
}
CORE_SWAP = [(0, 1), (1, 0)]

GATHER_ORDERS = [("z0", "z1"), ("z1", "z0")]
HALVING = [
    ("x0", "z0", "z1"),
    ("y0", "z1", "z0"),
    ("x0", "z0", "z1"),
    ("y0", "z1", "z0"),
    ("x1", "z0", "z1"),
    ("y1", "z1", "z0"),
]
GROUPS = [
    ((0, 2), ("x1", "y1", "y0"), "x0"),
    ((1, 3), ("y1", "x1", "x0"), "y0"),
    ((4,), ("y0", "x0", "y1"), "x1"),
    ((5,), ("x0", "y0", "x1"), "y1"),
]
WIDTH = HEADS_CORE * HDIM
ROWS = 2 * BLOCK
VMEM = pl.BlockSpec(memory_space=pltpu.VMEM)
barrier = lax.optimization_barrier


def swap(x, dim):
    if dim == "c":
        return lax.ppermute(x, "c", CORE_SWAP)
    return lax.ppermute(x, dim[0], PAIRS[dim[1]])


def gray(place):
    return place ^ (place >> 1)


def place_bit(dim):
    code = gray(lax.axis_index(dim[0]))
    return (code >> int(dim[1])) & 1


def colour():
    return (lax.axis_index("x") + lax.axis_index("y")) & 1


def block_order():
    blocks = []
    for i in range(8):
        code = gray(lax.axis_index("z")) ^ (i >> 2) ^ (((i >> 1) & 1) << 1)
        blocks.append(2 * (code ^ (code >> 1)) + (colour() ^ (i & 1)))
    return jnp.stack(blocks).astype(jnp.int32)


def dot(a, b, ca, cb):
    return lax.dot_general(a, b, (((ca,), (cb,)), ((), ())), preferred_element_type=F32)


def causal(x):
    rows = lax.broadcasted_iota(jnp.int32, x.shape, 0)
    cols = lax.broadcasted_iota(jnp.int32, x.shape, 1)
    return jnp.where(rows >= cols, x, 0.0).astype(BF)


def shape(dims, dtype):
    return jax.ShapeDtypeStruct(dims, dtype)


def prepare_kernel(core, *refs):
    for out, parts in ((refs[7], refs[:3]), (refs[8], refs[3:6])):
        for t in range(HEADS_CORE):
            for u in range(3):
                kind, head = place_of(t, u)
                out[t, :, u * HDIM : (u + 1) * HDIM] = parts[kind][:, cols(head)].astype(BF)
    refs[9][...] = refs[6][...]


def place_of(chunk, slot):
    place = 3 * (chunk % 2) + slot
    return place // 2, 2 * (chunk // 2) + place % 2


def cols(h):
    return slice(h * HDIM, (h + 1) * HDIM)


def prepare(core, master, cot):
    def spec(j, other):
        def index(i, c):
            return i, 2 * j + (1 - c[0] if other else c[0])

        return pl.BlockSpec((128, WIDTH), index)

    out = pl.BlockSpec((HEADS_CORE, 128, 3 * HDIM), lambda i, c: (0, i, 0))
    return pl.pallas_call(
        prepare_kernel,
        name="prepare",
        grid_spec=pltpu.PrefetchScalarGridSpec(
            num_scalar_prefetch=1,
            grid=(2,),
            in_specs=[spec(j, other) for other in (False, True) for j in range(3)]
            + [pl.BlockSpec((256, WIDTH), lambda i, c: (i, 1 - c[0]))],
            out_specs=(out, out, pl.BlockSpec((256, WIDTH), lambda i, c: (i, 0))),
        ),
        out_shape=(shape((HEADS_CORE, 256, 3 * HDIM), BF),) * 2 + (shape((BLOCK, WIDTH), BF),),
    )(core.reshape(1), *([master] * 6), cot)


def arrange_kernel(blocks, own, other, out):
    out[:BLOCK, :] = own[...]
    out[BLOCK:, :] = other[...]


def arrange(blocks, own, other):
    tile = pl.BlockSpec((BLOCK, 256), lambda i, b: (0, b[i]))
    return pl.pallas_call(
        arrange_kernel,
        name="arrange",
        grid_spec=pltpu.PrefetchScalarGridSpec(
            num_scalar_prefetch=1,
            grid=(8,),
            in_specs=[tile, tile],
            out_specs=pl.BlockSpec((ROWS, 256), lambda i, b: (0, i)),
        ),
        out_shape=shape((ROWS, own.shape[1]), BF),
    )(blocks, own, other)


def outer_kernel(k0, v0, k1, v1, kv):
    for pair, (keys, values) in enumerate(((k0, v0), (k1, v1))):
        for h in range(2):
            kv[2 * pair + h, 0] = dot(keys[:, cols(h)], values[:, cols(h)], 0, 0)


def own_states(first, second):
    keys = pl.BlockSpec((BLOCK, 256), lambda s: (s, 1))
    values = pl.BlockSpec((BLOCK, 256), lambda s: (s, 2))
    return pl.pallas_call(
        outer_kernel,
        name="outer",
        grid=(2,),
        in_specs=[keys, values, keys, values],
        out_specs=pl.BlockSpec((HEADS_CORE, 1, HDIM, HDIM), lambda s: (0, s, 0, 0)),
        out_shape=shape((HEADS_CORE, 2, HDIM, HDIM), F32),
    )(first, first, second, second)


def project(tokens, pieces):
    chunks = []
    for h, order in enumerate(GATHER_ORDERS):
        mine, low, high = pieces[3 * h : 3 * h + 3]
        theirs = (low, high)
        rows = []
        for i in range(8):
            flips = {"z0": i >> 2, "z1": (i >> 1) & 1}
            place = flips[order[0]] + 2 * flips[order[1]]
            rows.append(theirs[place // 2][place % 2] if i & 1 else mine[place])
        chunks.append(jnp.concatenate(rows, 0))
    weights = jnp.concatenate(chunks, 1)
    return jnp.dot(tokens, weights, preferred_element_type=F32).astype(BF)


def lower_scores(a, b):
    low = dot(a[256:], b, 1, 1)
    return causal(dot(a[:256], b[:256], 1, 1)), low[:, :256].astype(BF), causal(low[:, 256:])


def times(scores, x):
    first, left, right = scores
    low = jnp.concatenate([left, right], 1)
    return jnp.concatenate([dot(first, x[:256], 1, 0), dot(low, x, 1, 0)], 0)


def turned_times(scores, x):
    first, left, right = scores
    column = jnp.concatenate([first, left], 0)
    return jnp.concatenate([dot(column, x, 0, 0), dot(right, x[256:], 0, 0)], 0)


def running_kernel(received, out):
    total = jnp.zeros(received.shape[1:], F32)
    for place in range(received.shape[0]):
        out[place] = total.astype(BF)
        total = total + received[place]


def earlier_states(kv):
    cut = kv.reshape(16, -1, HDIM)
    received = lax.all_to_all(cut, ("x", "y"), 0, 0, tiled=True)
    sums = pl.pallas_call(
        running_kernel,
        name="running",
        out_shape=shape(received.shape, BF),
        in_specs=[VMEM],
        out_specs=VMEM,
    )(received)
    return lax.all_to_all(sums, ("x", "y"), 0, 0, tiled=True).reshape(kv.shape)


def head_of(ref, h, kind):
    return ref[:, pl.ds(pl.multiple_of((2 * "qkv".index(kind) + h) * HDIM, HDIM), HDIM)]


def head_cols(h):
    return pl.ds(pl.multiple_of(h * HDIM, HDIM), HDIM)


def each_head(body):
    def one(h, carry):
        body(h)
        return carry

    lax.fori_loop(0, 2, one, 0)


def pair_specs():
    qkv_rows = (BLOCK, 6 * HDIM)
    return [
        pl.BlockSpec(qkv_rows, lambda p, s, *_: (jnp.where(p == 0, s, 1), 0)),
        pl.BlockSpec(qkv_rows, lambda p, s, *_: (jnp.where(p == 0, 0, s), 0)),
    ]


def head_rows():
    return pl.BlockSpec((BLOCK, 256), lambda p, s, *_: (s, p))


def pick(first, second, h, kinds):
    pair = pl.program_id(0)
    return [jnp.where(pair == 0, head_of(first, h, j), head_of(second, h, j)) for j in kinds]


def within_kernel(first, second, out):
    @each_head
    def _(h):
        q, k, v = pick(first, second, h, "qkv")
        out[:, head_cols(h)] = times(lower_scores(q, k), v)


def local_scores(first, second):
    return pl.pallas_call(
        within_kernel,
        name="within",
        grid=(2, 2),
        in_specs=pair_specs(),
        out_specs=head_rows(),
        out_shape=shape((ROWS, WIDTH), F32),
    )(first, second)


def forward_kernel(core, first, second, within, state, cot_own, cot_other, attended, grad, qg):
    s = pl.program_id(1)

    @each_head
    def _(h):
        (q,) = pick(first, second, h, "q")
        at = head_cols(h)
        mixed = within[:, at] + dot(q, state[h, 0], 1, 0)
        inverse = lax.rsqrt(jnp.mean(mixed * mixed, -1, keepdims=True) + EPS_NORM)
        normed = mixed * inverse
        attended[:, at] = normed.astype(BF)
        out_grad = jnp.where(s == 0, cot_own[:, at], cot_other[:, at]).astype(F32)
        along = jnp.mean(out_grad * normed, -1, keepdims=True)
        g = (inverse * (out_grad - normed * along)).astype(BF)
        grad[:, at] = g
        qg[h, 0] = dot(q, g, 0, 0).astype(BF)


def forward(core, first, second, within, state, cot_own, cot_other):
    rows = head_rows()
    states = pl.BlockSpec((2, 1, HDIM, HDIM), lambda p, s, c: (p, s, 0, 0))
    queries = (BLOCK, 2 * HDIM)
    return pl.pallas_call(
        forward_kernel,
        name="forward",
        grid_spec=pltpu.PrefetchScalarGridSpec(
            num_scalar_prefetch=1,
            grid=(2, 2),
            in_specs=[
                pl.BlockSpec(queries, lambda p, s, c: (jnp.where(p == 0, s, 1), 0)),
                pl.BlockSpec(queries, lambda p, s, c: (jnp.where(p == 0, 0, s), 0)),
                rows,
                states,
                pl.BlockSpec((BLOCK, 256), lambda p, s, c: (0, 2 * c[0] + p)),
                pl.BlockSpec((BLOCK, 256), lambda p, s, c: (0, p)),
            ],
            out_specs=(rows, rows, states),
        ),
        out_shape=(
            shape((ROWS, WIDTH), BF),
            shape((ROWS, WIDTH), BF),
            shape((HEADS_CORE, 2, HDIM, HDIM), BF),
        ),
    )(core.reshape(1), first, second, within, state, cot_own, cot_other)


def backward_kernel(pair, qkv, grad, state, dq, dkv):
    for h in range(2):
        q, k, v = [qkv[:, cols(2 * j + h)] for j in range(3)]
        at = cols(h)
        g = grad[:, at]
        back = lower_scores(g, v)
        dq[:, at] = (times(back, k) + dot(g, state[h, 0], 1, 1)).astype(BF)
        dkv[0, :, at] = turned_times(back, q)
        dkv[1, :, at] = turned_times(lower_scores(q, k), g)


def backward(pair, qkv, grad, state):
    return pl.pallas_call(
        backward_kernel,
        name="backward",
        grid_spec=pltpu.PrefetchScalarGridSpec(
            num_scalar_prefetch=1,
            grid=(2,),
            in_specs=[
                pl.BlockSpec((BLOCK, 6 * HDIM), lambda s, p: (s, 0)),
                pl.BlockSpec((BLOCK, 256), lambda s, p: (s, p[0])),
                pl.BlockSpec((2, 1, HDIM, HDIM), lambda s, p: (p[0], s, 0, 0)),
            ],
            out_specs=(
                pl.BlockSpec((BLOCK, 256), lambda s, p: (s, 0)),
                pl.BlockSpec((2, BLOCK, 256), lambda s, p: (0, s, 0)),
            ),
        ),
        out_shape=(shape((ROWS, 256), BF), shape((2, ROWS, 256), F32)),
    )(jnp.full((1,), pair, jnp.int32), qkv, grad, state)


def token_copy(i, tokens, held, sems):
    at = pl.ds(pl.multiple_of(i * 512, 512), 512)
    return pltpu.make_async_copy(tokens.at[:, at], held.at[:, at], sems.at[i])


def fetch_tokens(tokens, held, sems):
    for i in range(4):
        token_copy(i, tokens, held, sems).start()


def multiply_blocks(keeps, offset, turned, held, arriving, outs):
    def blocks(i, carry):
        if arriving is not None:
            token_copy(i, *arriving).wait()
        at = pl.ds(pl.multiple_of(i * 512, 512), 512)
        piece = dot(turned[...], held[:, at], 1, 0).astype(BF)
        for part in range(2):
            sent, kept = outs[2 * part], outs[2 * part + 1]
            first = piece[part * 256 : (part + 1) * 256, :256]
            second = piece[part * 256 : (part + 1) * 256, 256:]
            straight = keeps[offset + part] == 0
            kept[i] = jnp.where(straight, first, second)
            sent[i] = jnp.where(straight, second, first)
        return carry

    lax.fori_loop(0, 4, blocks, 0)


def query_gradient_kernel(keeps, q0, q1, tokens, s0, k0, s1, k1, turned, held, sems):
    fetch_tokens(tokens, held, sems)
    turned[:256, :] = q0[...].T
    turned[256:, :] = q1[...].T
    multiply_blocks(keeps, 0, turned, held, (tokens, held, sems), (s0, k0, s1, k1))


def gradient_kernel(keeps, k0, v0, k1, v1, d0, d1, state, tokens, *refs):
    outs, (turned, held, sems) = refs[:8], refs[8:]
    fetch_tokens(tokens, held, sems)
    for kind in range(2):
        sides = ((v0 if kind == 0 else k0, d0), (v1 if kind == 0 else k1, d1))
        for pair, (source, within) in enumerate(sides):

            @each_head
            def _(h):
                head = 2 * pair + h
                at = head_cols(h)
                for s in range(2):
                    span = slice(s * BLOCK, (s + 1) * BLOCK)
                    later = dot(source[span, at], state[head, s], 1, 1 - kind)
                    total = within[kind, span, at] + later
                    turned[head_cols(head), span] = total.astype(BF).T

        arriving = (tokens, held, sems) if kind == 0 else None
        multiply_blocks(keeps, 2 * kind, turned, held, arriving, outs[4 * kind : 4 * kind + 4])


def gradient_call(kernel, first, ins, specs, tokens):
    count = len(first)
    keeps = jnp.stack([colour() ^ place_bit(HALVING[p][0]) for p in first]).astype(jnp.int32)
    return pl.pallas_call(
        kernel,
        grid=(1,),
        in_specs=[pl.BlockSpec(memory_space=pltpu.SMEM)]
        + specs
        + [pl.BlockSpec(memory_space=pl.ANY)],
        out_specs=(VMEM,) * (2 * count),
        out_shape=(shape((4, 256, 256), BF),) * (2 * count),
        scratch_shapes=[
            pltpu.VMEM((WIDTH, ROWS), BF),
            pltpu.VMEM((ROWS, 2048), BF),
            pltpu.SemaphoreType.DMA((4,)),
        ],
    )(keeps, *ins, tokens)


def query_gradient(q0, q1, tokens):
    return gradient_call(query_gradient_kernel, (0, 1), (q0, q1), [VMEM] * 2, tokens)


def key_value_gradient(first, second, d_first, d_second, state, tokens):
    specs = [pl.BlockSpec((ROWS, 256), lambda _, j=j: (0, j)) for j in (1, 2)] * 2 + [VMEM] * 3
    ins = (first, first, second, second, d_first, d_second, state)
    return gradient_call(gradient_kernel, (2, 3, 4, 5), ins, specs, tokens)


def wide(x):
    return x.astype(F32)


def add(a, b):
    return (wide(a) + wide(b)).astype(BF)


def reduce_part(sent, kept, order):
    received = swap(sent, order[0])
    part = add(kept, received).reshape(2, 2, 256, 256)
    for i, dim in enumerate(order[1:]):
        axis = int(dim[1]) if i == 0 else 0
        send = lax.index_in_dim(part, 1, axis, False)
        part = add(lax.index_in_dim(part, 0, axis, False), swap(send, dim))
    return part


def finish_group(parts, exchanged, last):
    total = jnp.stack(parts)
    for dim in exchanged:
        total = add(total, swap(total, dim))
    return total, swap(total, last)


def later_steps(total, later):
    total = wide(total)
    carried = jnp.zeros_like(total)
    for dim in ("y0", "y1", "x0", "x1"):
        moving = swap(total.astype(BF), dim)
        received = yield moving
        received = wide(received)
        upper = (lax.axis_index(dim[0]) >> int(dim[1])) & 1
        carried = carried + jnp.where(upper == (0 if later else 1), received, 0.0)
        total = total + received
    yield carried.astype(BF)


def sort_kernel(holds, *refs):
    kept, sent = refs[-2:]
    for g, (members, _, _) in enumerate(GROUPS):
        straight = holds[g] == 1
        for j, p in enumerate(members):
            at = slice(p * 256, (p + 1) * 256)
            here, there = refs[2 * g][j], refs[2 * g + 1][j]
            kept[:, at] = jnp.where(straight, here, there).T
            sent[:, at] = jnp.where(straight, there, here).T


def sort_pieces(holds, finished):
    return pl.pallas_call(
        sort_kernel,
        name="sort_pieces",
        in_specs=[pl.BlockSpec(memory_space=pltpu.SMEM)] + [VMEM] * len(finished),
        out_specs=(VMEM, VMEM),
        out_shape=(shape((256, 3 * WIDTH), BF),) * 2,
    )(holds, *finished)


def join_kernel(core, own, other, out):
    straight = core[0] == 0
    out[0, :, :WIDTH] = jnp.where(straight, own[...], other[...])
    out[0, :, WIDTH:] = jnp.where(straight, other[...], own[...])


def join_heads(core, own, other):
    half = pl.BlockSpec((256, WIDTH), lambda i, c: (i, 0))
    return pl.pallas_call(
        join_kernel,
        name="join_heads",
        grid_spec=pltpu.PrefetchScalarGridSpec(
            num_scalar_prefetch=1,
            grid=(2,),
            in_specs=[half, half],
            out_specs=pl.BlockSpec((1, 256, 2 * WIDTH), lambda i, c: (0, i, 0)),
        ),
        out_shape=shape((1, BLOCK, 2 * WIDTH), BF),
    )(core.reshape(1), own, other)


def adam(core, kept, received, weights, first, second):
    pieces = []
    for kind in range(3):
        at = slice(kind * WIDTH, (kind + 1) * WIDTH)
        pieces.append(jnp.where(core == 0, kept[:, at], received[:, at]))
        pieces.append(jnp.where(core == 0, received[:, at], kept[:, at]))
    gradient = jnp.concatenate(pieces, 1).astype(F32)
    new_first = BETA_ONE * first + (1.0 - BETA_ONE) * gradient
    new_second = BETA_TWO * second + (1.0 - BETA_TWO) * gradient * gradient
    first_hat = new_first * (1.0 / (1.0 - BETA_ONE**STEP))
    second_hat = new_second * (1.0 / (1.0 - BETA_TWO**STEP))
    new_weights = weights - LEARN_RATE * (
        first_hat / (jnp.sqrt(second_hat) + EPS_ADAM) + DECAY_WEIGHT * weights
    )
    return new_weights, new_first, new_second


def gather_step(step, mine):
    got = []
    for h in range(2):
        got.append(swap(mine[h], GATHER_ORDERS[h][step]))
    return [jnp.concatenate([mine[h], got[h]], 0) for h in range(2)]


def exchange_colours(mine):
    pieces = []
    for h, axis in enumerate("xy"):
        pieces.append(mine[h])
        for side in range(2):
            pieces.append(swap(mine[h][2 * side : 2 * side + 2], f"{axis}{side}"))
    return pieces


def step(tokens, weights_master, adam_first, adam_second, cotangent):
    core = lax.axis_index("c")
    own = tokens[0]
    straight = colour() == core

    held, outgoing, cot_out = prepare(core, weights_master, cotangent[0])
    traded = swap(outgoing, "c")
    other = swap(own, "c")
    cot_other = swap(cot_out, "c")

    blocks = block_order()
    mine = jnp.where(straight, held, traded)
    first = gather_step(0, [mine[0][None], mine[1][None]])
    first = gather_step(1, first)
    both = arrange(blocks, own, other)
    first, mine, both = barrier((first, mine, both))
    pieces = exchange_colours(first)
    second = gather_step(0, [mine[2][None], mine[3][None]])
    second = gather_step(1, second)
    qkv_first = project(both, pieces)
    second, qkv_first = barrier((second, qkv_first))
    qkv_second = project(both, exchange_colours(second))

    state = earlier_states(own_states(qkv_first, qkv_second))
    within = local_scores(qkv_first, qkv_second)
    attended, grad, qg = forward(
        core, qkv_first, qkv_second, within, state, cotangent[0], cot_other
    )

    steps = later_steps(qg, True)
    received = next(steps)
    q0, d0 = backward(0, qkv_first, grad, state)
    received, q0, d0, grad = barrier((received, q0, d0, grad))
    received = steps.send(received)
    q1, d1 = backward(1, qkv_second, grad, state)
    received, q0, q1, d1 = barrier((received, q0, q1, d1))
    received = steps.send(received)
    parts = query_gradient(q0, q1, both)
    received, parts = barrier((received, parts))
    received = steps.send(received)
    later = steps.send(received)
    parts += key_value_gradient(qkv_first, qkv_second, d0, d1, later, both)
    reduced = [
        reduce_part(parts[2 * p], parts[2 * p + 1], order) for p, order in enumerate(HALVING)
    ]

    attended_other = swap(attended[BLOCK:], "c")
    attended_out = join_heads(core, attended, attended_other)

    holds, finished = [], []
    for members, exchanged, last in GROUPS:
        holds.append(place_bit(last) == core)
        finished += finish_group([reduced[p] for p in members], exchanged, last)
    kept, sent = sort_pieces(jnp.stack(holds).astype(jnp.int32), finished)
    received = swap(sent, "c")
    new_weights, new_first, new_second = adam(
        core, kept, received, weights_master, adam_first, adam_second
    )
    return (attended_out, new_weights, new_first, new_second)


def solution(mesh):
    torus = Mesh(mesh.devices.reshape(4, 4, 4, 2), ("x", "y", "z", "c"))
    rows = P(("z", "c"), ("x", "y"), None)
    shard = P(("z", "c"), None)
    return jax.shard_map(
        step,
        mesh=torus,
        in_specs=(rows, shard, shard, shard, rows),
        out_specs=(rows, shard, shard, shard),
        check_vma=False,
    )
```

```python
import jax
import jax.numpy as jnp
from jax import lax
from jax.experimental import pallas as pl
from jax.experimental.pallas import tpu as pltpu
from jax.sharding import Mesh, PartitionSpec as P


HDIM = 128
BLOCK = 512
STEP = 100
HEADS_CORE = 4

EPS_NORM = 1e-05
BETA_ONE = 0.9
BETA_TWO = 0.95
LEARN_RATE = 0.001
DECAY_WEIGHT = 0.1
EPS_ADAM = 1e-08

BF = jnp.bfloat16
F32 = jnp.float32


PAIRS = {
    "0": [(0, 1), (1, 0), (2, 3), (3, 2)],
    "1": [(1, 2), (2, 1), (3, 0), (0, 3)],
}
CORE_SWAP = [(0, 1), (1, 0)]

GATHER_ORDERS = [("z0", "z1"), ("z1", "z0")]
HALVING = [
    ("z0", "x0", "z1"),
    ("z1", "y0", "z0"),
    ("x1", "z0", "z1"),
    ("y1", "z1", "z0"),
    ("z0", "x0", "z1"),
    ("z1", "y0", "z0"),
]
GROUPS = [
    ((0, 4), ("x1", "y1", "y0"), "x0"),
    ((1, 5), ("y1", "x1", "x0"), "y0"),
    ((2,), ("y0", "x0", "y1"), "x1"),
    ((3,), ("x0", "y0", "x1"), "y1"),
]
WIDTH = HEADS_CORE * HDIM
ROWS = 2 * BLOCK
VMEM = pl.BlockSpec(memory_space=pltpu.VMEM)
barrier = lax.optimization_barrier


def swap(x, dim):
    if dim == "c":
        return lax.ppermute(x, "c", CORE_SWAP)
    return lax.ppermute(x, dim[0], PAIRS[dim[1]])


def gray(place):
    return place ^ (place >> 1)


def place_bit(dim):
    code = gray(lax.axis_index(dim[0]))
    return (code >> int(dim[1])) & 1


def colour():
    return (lax.axis_index("x") + lax.axis_index("y")) & 1


def block_order():
    blocks = []
    for i in range(8):
        code = gray(lax.axis_index("z")) ^ (i >> 2) ^ (((i >> 1) & 1) << 1)
        blocks.append(2 * (code ^ (code >> 1)) + (colour() ^ (i & 1)))
    return jnp.stack(blocks).astype(jnp.int32)


def dot(a, b, ca, cb):
    return lax.dot_general(a, b, (((ca,), (cb,)), ((), ())), preferred_element_type=F32)


def causal(x):
    rows = lax.broadcasted_iota(jnp.int32, x.shape, 0)
    cols = lax.broadcasted_iota(jnp.int32, x.shape, 1)
    return jnp.where(rows >= cols, x, 0.0).astype(BF)


def shape(dims, dtype):
    return jax.ShapeDtypeStruct(dims, dtype)


def prepare_kernel(core, *refs):
    for out, parts in ((refs[7], refs[:3]), (refs[8], refs[3:6])):
        for t in range(HEADS_CORE):
            for u in range(3):
                kind, head = place_of(t, u)
                out[t, :, u * HDIM : (u + 1) * HDIM] = parts[kind][:, cols(head)].astype(BF)
    refs[9][...] = refs[6][...]


def place_of(chunk, slot):
    place = 3 * (chunk % 2) + slot
    return place // 2, 2 * (chunk // 2) + place % 2


def cols(h):
    return slice(h * HDIM, (h + 1) * HDIM)


def prepare(core, master, cot):
    def spec(j, other):
        def index(i, c):
            return i, 2 * j + (1 - c[0] if other else c[0])

        return pl.BlockSpec((128, WIDTH), index)

    out = pl.BlockSpec((HEADS_CORE, 128, 3 * HDIM), lambda i, c: (0, i, 0))
    return pl.pallas_call(
        prepare_kernel,
        name="prepare",
        grid_spec=pltpu.PrefetchScalarGridSpec(
            num_scalar_prefetch=1,
            grid=(2,),
            in_specs=[spec(j, other) for other in (False, True) for j in range(3)]
            + [pl.BlockSpec((256, WIDTH), lambda i, c: (i, 1 - c[0]))],
            out_specs=(out, out, pl.BlockSpec((256, WIDTH), lambda i, c: (i, 0))),
        ),
        out_shape=(shape((HEADS_CORE, 256, 3 * HDIM), BF),) * 2 + (shape((BLOCK, WIDTH), BF),),
    )(core.reshape(1), *([master] * 6), cot)


def arrange_kernel(blocks, own, other, out):
    out[:BLOCK, :] = own[...]
    out[BLOCK:, :] = other[...]


def arrange(blocks, own, other):
    tile = pl.BlockSpec((BLOCK, 256), lambda i, b: (0, b[i]))
    return pl.pallas_call(
        arrange_kernel,
        name="arrange",
        grid_spec=pltpu.PrefetchScalarGridSpec(
            num_scalar_prefetch=1,
            grid=(8,),
            in_specs=[tile, tile],
            out_specs=pl.BlockSpec((ROWS, 256), lambda i, b: (0, i)),
        ),
        out_shape=shape((ROWS, own.shape[1]), BF),
    )(blocks, own, other)


def outer_kernel(k0, v0, k1, v1, kv):
    for pair, (keys, values) in enumerate(((k0, v0), (k1, v1))):
        for h in range(2):
            kv[2 * pair + h, 0] = dot(keys[:, cols(h)], values[:, cols(h)], 0, 0)


def own_states(first, second):
    keys = pl.BlockSpec((BLOCK, 256), lambda s: (s, 1))
    values = pl.BlockSpec((BLOCK, 256), lambda s: (s, 2))
    return pl.pallas_call(
        outer_kernel,
        name="outer",
        grid=(2,),
        in_specs=[keys, values, keys, values],
        out_specs=pl.BlockSpec((HEADS_CORE, 1, HDIM, HDIM), lambda s: (0, s, 0, 0)),
        out_shape=shape((HEADS_CORE, 2, HDIM, HDIM), F32),
    )(first, first, second, second)


def project(tokens, pieces):
    chunks = []
    for h, order in enumerate(GATHER_ORDERS):
        mine, low, high = pieces[3 * h : 3 * h + 3]
        theirs = (low, high)
        rows = []
        for i in range(8):
            flips = {"z0": i >> 2, "z1": (i >> 1) & 1}
            place = flips[order[0]] + 2 * flips[order[1]]
            rows.append(theirs[place // 2][place % 2] if i & 1 else mine[place])
        chunks.append(jnp.concatenate(rows, 0))
    weights = jnp.concatenate(chunks, 1)
    return jnp.dot(tokens, weights, preferred_element_type=F32).astype(BF)


def lower_scores(a, b):
    low = dot(a[256:], b, 1, 1)
    return causal(dot(a[:256], b[:256], 1, 1)), low[:, :256].astype(BF), causal(low[:, 256:])


def times(scores, x):
    first, left, right = scores
    low = jnp.concatenate([left, right], 1)
    return jnp.concatenate([dot(first, x[:256], 1, 0), dot(low, x, 1, 0)], 0)


def turned_times(scores, x):
    first, left, right = scores
    column = jnp.concatenate([first, left], 0)
    return jnp.concatenate([dot(column, x, 0, 0), dot(right, x[256:], 0, 0)], 0)


def running_kernel(received, out):
    total = jnp.zeros(received.shape[1:], F32)
    for place in range(received.shape[0]):
        out[place] = total.astype(BF)
        total = total + received[place]


def earlier_states(kv):
    cut = kv.reshape(16, -1, HDIM)
    received = lax.all_to_all(cut, ("x", "y"), 0, 0, tiled=True)
    sums = pl.pallas_call(
        running_kernel,
        name="running",
        out_shape=shape(received.shape, BF),
        in_specs=[VMEM],
        out_specs=VMEM,
    )(received)
    return lax.all_to_all(sums, ("x", "y"), 0, 0, tiled=True).reshape(kv.shape)


def head_of(ref, h, kind):
    return ref[:, pl.ds(pl.multiple_of((2 * "qkv".index(kind) + h) * HDIM, HDIM), HDIM)]


def head_cols(h):
    return pl.ds(pl.multiple_of(h * HDIM, HDIM), HDIM)


def each_head(body):
    def one(h, carry):
        body(h)
        return carry

    lax.fori_loop(0, 2, one, 0)


def pair_specs():
    qkv_rows = (BLOCK, 6 * HDIM)
    return [
        pl.BlockSpec(qkv_rows, lambda p, s, *_: (jnp.where(p == 0, s, 1), 0)),
        pl.BlockSpec(qkv_rows, lambda p, s, *_: (jnp.where(p == 0, 0, s), 0)),
    ]


def head_rows():
    return pl.BlockSpec((BLOCK, 256), lambda p, s, *_: (s, p))


def pick(first, second, h, kinds):
    pair = pl.program_id(0)
    return [jnp.where(pair == 0, head_of(first, h, j), head_of(second, h, j)) for j in kinds]


def within_kernel(first, second, out):
    @each_head
    def _(h):
        q, k, v = pick(first, second, h, "qkv")
        out[:, head_cols(h)] = times(lower_scores(q, k), v)


def local_scores(first, second):
    return pl.pallas_call(
        within_kernel,
        name="within",
        grid=(2, 2),
        in_specs=pair_specs(),
        out_specs=head_rows(),
        out_shape=shape((ROWS, WIDTH), F32),
    )(first, second)


def forward_kernel(core, first, second, within, state, cot_own, cot_other, attended, grad, qg):
    s = pl.program_id(1)

    @each_head
    def _(h):
        (q,) = pick(first, second, h, "q")
        at = head_cols(h)
        mixed = within[:, at] + dot(q, state[h, 0], 1, 0)
        inverse = lax.rsqrt(jnp.mean(mixed * mixed, -1, keepdims=True) + EPS_NORM)
        normed = mixed * inverse
        attended[:, at] = normed.astype(BF)
        out_grad = jnp.where(s == 0, cot_own[:, at], cot_other[:, at]).astype(F32)
        along = jnp.mean(out_grad * normed, -1, keepdims=True)
        g = (inverse * (out_grad - normed * along)).astype(BF)
        grad[:, at] = g
        qg[h, 0] = dot(q, g, 0, 0).astype(BF)


def forward(core, first, second, within, state, cot_own, cot_other):
    rows = head_rows()
    states = pl.BlockSpec((2, 1, HDIM, HDIM), lambda p, s, c: (p, s, 0, 0))
    queries = (BLOCK, 2 * HDIM)
    return pl.pallas_call(
        forward_kernel,
        name="forward",
        grid_spec=pltpu.PrefetchScalarGridSpec(
            num_scalar_prefetch=1,
            grid=(2, 2),
            in_specs=[
                pl.BlockSpec(queries, lambda p, s, c: (jnp.where(p == 0, s, 1), 0)),
                pl.BlockSpec(queries, lambda p, s, c: (jnp.where(p == 0, 0, s), 0)),
                rows,
                states,
                pl.BlockSpec((BLOCK, 256), lambda p, s, c: (0, 2 * c[0] + p)),
                pl.BlockSpec((BLOCK, 256), lambda p, s, c: (0, p)),
            ],
            out_specs=(rows, rows, states),
        ),
        out_shape=(
            shape((ROWS, WIDTH), BF),
            shape((ROWS, WIDTH), BF),
            shape((HEADS_CORE, 2, HDIM, HDIM), BF),
        ),
    )(core.reshape(1), first, second, within, state, cot_own, cot_other)


def backward_kernel(pair, qkv, grad, state, dq, dkv):
    for h in range(2):
        q, k, v = [qkv[:, cols(2 * j + h)] for j in range(3)]
        at = cols(h)
        g = grad[:, at]
        back = lower_scores(g, v)
        dq[:, at] = (times(back, k) + dot(g, state[h, 0], 1, 1)).astype(BF)
        dkv[0, :, at] = turned_times(back, q)
        dkv[1, :, at] = turned_times(lower_scores(q, k), g)


def backward(pair, qkv, grad, state):
    return pl.pallas_call(
        backward_kernel,
        name="backward",
        grid_spec=pltpu.PrefetchScalarGridSpec(
            num_scalar_prefetch=1,
            grid=(2,),
            in_specs=[
                pl.BlockSpec((BLOCK, 6 * HDIM), lambda s, p: (s, 0)),
                pl.BlockSpec((BLOCK, 256), lambda s, p: (s, p[0])),
                pl.BlockSpec((2, 1, HDIM, HDIM), lambda s, p: (p[0], s, 0, 0)),
            ],
            out_specs=(
                pl.BlockSpec((BLOCK, 256), lambda s, p: (s, 0)),
                pl.BlockSpec((2, BLOCK, 256), lambda s, p: (0, s, 0)),
            ),
        ),
        out_shape=(shape((ROWS, 256), BF), shape((2, ROWS, 256), F32)),
    )(jnp.full((1,), pair, jnp.int32), qkv, grad, state)


def token_copy(i, tokens, held, sems):
    at = pl.ds(pl.multiple_of(i * 512, 512), 512)
    return pltpu.make_async_copy(tokens.at[:, at], held.at[:, at], sems.at[i])


def fetch_tokens(tokens, held, sems):
    for i in range(4):
        token_copy(i, tokens, held, sems).start()


def multiply_blocks(first, keeps, turned, held, arriving, outs):
    def blocks(i, carry):
        if arriving is not None:
            token_copy(i, *arriving).wait()
        at = pl.ds(pl.multiple_of(i * 512, 512), 512)
        piece = dot(turned[...], held[:, at], 1, 0).astype(BF)
        for part in range(2):
            sent, kept = outs[2 * part], outs[2 * part + 1]
            even = piece[part * 256 : (part + 1) * 256, :256]
            odd = piece[part * 256 : (part + 1) * 256, 256:]
            dim = HALVING[first + part][0]
            if dim[0] != "z":
                straight = keeps[part] == 0
                kept[i] = jnp.where(straight, even, odd)
                sent[i] = jnp.where(straight, odd, even)
                continue
            bits = (i >> 1, i & 1)
            moves, place = bits[int(dim[1])], 2 * bits[1 - int(dim[1])]

            @pl.when(moves == 1)
            def _():
                sent[place] = even
                sent[place + 1] = odd

            @pl.when(moves == 0)
            def _():
                kept[place] = even
                kept[place + 1] = odd

        return carry

    lax.fori_loop(0, 4, blocks, 0)


def query_gradient_kernel(keeps, q0, q1, tokens, s0, k0, s1, k1, turned, held, sems):
    fetch_tokens(tokens, held, sems)
    turned[:256, :] = q0[...].T
    turned[256:, :] = q1[...].T
    multiply_blocks(0, keeps, turned, held, (tokens, held, sems), (s0, k0, s1, k1))


def gradient_kernel(keeps, k0, v0, k1, v1, d0, d1, state, tokens, *refs):
    outs, (turned, held, sems) = refs[:8], refs[8:]
    fetch_tokens(tokens, held, sems)
    for kind in range(2):
        sides = ((v0 if kind == 0 else k0, d0), (v1 if kind == 0 else k1, d1))
        for pair, (source, within) in enumerate(sides):

            @each_head
            def _(h):
                head = 2 * pair + h
                at = head_cols(h)
                for s in range(2):
                    span = slice(s * BLOCK, (s + 1) * BLOCK)
                    later = dot(source[span, at], state[head, s], 1, 1 - kind)
                    total = within[kind, span, at] + later
                    turned[head_cols(head), span] = total.astype(BF).T

        arriving = (tokens, held, sems) if kind == 0 else None
        multiply_blocks(2 + 2 * kind, keeps, turned, held, arriving, outs[4 * kind : 4 * kind + 4])


def gradient_call(kernel, first, ins, specs, tokens):
    count = len(first)
    keeps = jnp.stack([colour() ^ place_bit(HALVING[p][0]) for p in (2, 3)]).astype(jnp.int32)
    return pl.pallas_call(
        kernel,
        grid=(1,),
        in_specs=[pl.BlockSpec(memory_space=pltpu.SMEM)]
        + specs
        + [pl.BlockSpec(memory_space=pl.ANY)],
        out_specs=(VMEM,) * (2 * count),
        out_shape=(shape((4, 256, 256), BF),) * (2 * count),
        scratch_shapes=[
            pltpu.VMEM((WIDTH, ROWS), BF),
            pltpu.VMEM((ROWS, 2048), BF),
            pltpu.SemaphoreType.DMA((4,)),
        ],
    )(keeps, *ins, tokens)


def query_gradient(q0, q1, tokens):
    return gradient_call(query_gradient_kernel, (0, 1), (q0, q1), [VMEM] * 2, tokens)


def key_value_gradient(first, second, d_first, d_second, state, tokens):
    specs = [pl.BlockSpec((ROWS, 256), lambda _, j=j: (0, j)) for j in (1, 2)] * 2 + [VMEM] * 3
    ins = (first, first, second, second, d_first, d_second, state)
    return gradient_call(gradient_kernel, (2, 3, 4, 5), ins, specs, tokens)


def wide(x):
    return x.astype(F32)


def add(a, b):
    return (wide(a) + wide(b)).astype(BF)


def reduce_part(sent, kept, order):
    received = swap(sent, order[0])
    part = add(kept, received).reshape(2, 2, 256, 256)
    if order[0][0] == "z":
        keeps = colour() ^ place_bit(order[1])
        send = lax.dynamic_index_in_dim(part, 1 - keeps, 1, False)
        keep = lax.dynamic_index_in_dim(part, keeps, 1, False)
    else:
        send = lax.index_in_dim(part, 1, int(order[1][1]), False)
        keep = lax.index_in_dim(part, 0, int(order[1][1]), False)
    part = add(keep, swap(send, order[1]))
    return add(part[0], swap(part[1], order[2]))


def finish_group(parts, exchanged, last):
    total = jnp.stack(parts)
    for dim in exchanged:
        total = add(total, swap(total, dim))
    return total, swap(total, last)


def later_steps(total, later):
    total = wide(total)
    carried = jnp.zeros_like(total)
    for dim in ("y0", "y1", "x0", "x1"):
        moving = swap(total.astype(BF), dim)
        received = yield moving
        received = wide(received)
        upper = (lax.axis_index(dim[0]) >> int(dim[1])) & 1
        carried = carried + jnp.where(upper == (0 if later else 1), received, 0.0)
        total = total + received
    yield carried.astype(BF)


def sort_kernel(holds, *refs):
    kept, sent = refs[-2:]
    for g, (members, _, _) in enumerate(GROUPS):
        straight = holds[g] == 1
        for j, p in enumerate(members):
            at = slice(p * 256, (p + 1) * 256)
            here, there = refs[2 * g][j], refs[2 * g + 1][j]
            kept[:, at] = jnp.where(straight, here, there).T
            sent[:, at] = jnp.where(straight, there, here).T


def sort_pieces(holds, finished):
    return pl.pallas_call(
        sort_kernel,
        name="sort_pieces",
        in_specs=[pl.BlockSpec(memory_space=pltpu.SMEM)] + [VMEM] * len(finished),
        out_specs=(VMEM, VMEM),
        out_shape=(shape((256, 3 * WIDTH), BF),) * 2,
    )(holds, *finished)


def join_kernel(core, own, other, out):
    straight = core[0] == 0
    out[0, :, :WIDTH] = jnp.where(straight, own[...], other[...])
    out[0, :, WIDTH:] = jnp.where(straight, other[...], own[...])


def join_heads(core, own, other):
    half = pl.BlockSpec((256, WIDTH), lambda i, c: (i, 0))
    return pl.pallas_call(
        join_kernel,
        name="join_heads",
        grid_spec=pltpu.PrefetchScalarGridSpec(
            num_scalar_prefetch=1,
            grid=(2,),
            in_specs=[half, half],
            out_specs=pl.BlockSpec((1, 256, 2 * WIDTH), lambda i, c: (0, i, 0)),
        ),
        out_shape=shape((1, BLOCK, 2 * WIDTH), BF),
    )(core.reshape(1), own, other)


def adam_kernel(core, kept, received, weights, first, second, out_weights, out_first, out_second):
    for block in range(6):
        at = slice(block * WIDTH, (block + 1) * WIDTH)
        source = slice((block // 2) * WIDTH, (block // 2 + 1) * WIDTH)
        gradient = jnp.where(block % 2 == core[0], kept[:, source], received[:, source]).astype(F32)
        new_first = BETA_ONE * first[:, at] + (1.0 - BETA_ONE) * gradient
        new_second = BETA_TWO * second[:, at] + (1.0 - BETA_TWO) * gradient * gradient
        first_hat = new_first * (1.0 / (1.0 - BETA_ONE**STEP))
        second_hat = new_second * (1.0 / (1.0 - BETA_TWO**STEP))
        root = second_hat * lax.rsqrt(second_hat)
        out_first[:, at] = new_first
        out_second[:, at] = new_second
        out_weights[:, at] = weights[:, at] - LEARN_RATE * (
            first_hat * pl.reciprocal(root + EPS_ADAM) + DECAY_WEIGHT * weights[:, at]
        )


def adam(core, kept, received, *arrays):
    piece = pl.BlockSpec((32, 3 * WIDTH), lambda i, c: (i, 0))
    block = pl.BlockSpec((32, 6 * WIDTH), lambda i, c: (i, 0))
    return pl.pallas_call(
        adam_kernel,
        name="adam",
        grid_spec=pltpu.PrefetchScalarGridSpec(
            num_scalar_prefetch=1,
            grid=(8,),
            in_specs=[piece, piece, block, block, block],
            out_specs=(block,) * 3,
        ),
        out_shape=tuple(shape(x.shape, F32) for x in arrays),
    )(core.reshape(1), kept, received, *arrays)


def gather_step(step, mine):
    got = []
    for h in range(2):
        got.append(swap(mine[h], GATHER_ORDERS[h][step]))
    return [jnp.concatenate([mine[h], got[h]], 0) for h in range(2)]


def exchange_colours(mine):
    pieces = []
    for h, axis in enumerate("xy"):
        pieces.append(mine[h])
        for side in range(2):
            pieces.append(swap(mine[h][2 * side : 2 * side + 2], f"{axis}{side}"))
    return pieces


def step(tokens, weights_master, adam_first, adam_second, cotangent):
    core = lax.axis_index("c")
    own = tokens[0]
    straight = colour() == core

    held, outgoing, cot_out = prepare(core, weights_master, cotangent[0])
    traded = swap(outgoing, "c")
    other = swap(own, "c")
    cot_other = swap(cot_out, "c")

    blocks = block_order()
    mine = jnp.where(straight, held, traded)
    first = gather_step(0, [mine[0][None], mine[1][None]])
    first = gather_step(1, first)
    both = arrange(blocks, own, other)
    first, mine, both = barrier((first, mine, both))
    pieces = exchange_colours(first)
    second = gather_step(0, [mine[2][None], mine[3][None]])
    second = gather_step(1, second)
    qkv_first = project(both, pieces)
    second, qkv_first = barrier((second, qkv_first))
    qkv_second = project(both, exchange_colours(second))

    state = earlier_states(own_states(qkv_first, qkv_second))
    within = local_scores(qkv_first, qkv_second)
    attended, grad, qg = forward(
        core, qkv_first, qkv_second, within, state, cotangent[0], cot_other
    )

    steps = later_steps(qg, True)
    received = next(steps)
    q0, d0 = backward(0, qkv_first, grad, state)
    received, q0, d0, grad = barrier((received, q0, d0, grad))
    received = steps.send(received)
    q1, d1 = backward(1, qkv_second, grad, state)
    received, q0, q1, d1 = barrier((received, q0, q1, d1))
    received = steps.send(received)
    parts = query_gradient(q0, q1, both)
    received, parts = barrier((received, parts))
    received = steps.send(received)
    later = steps.send(received)
    parts += key_value_gradient(qkv_first, qkv_second, d0, d1, later, both)
    reduced = [
        reduce_part(parts[2 * p], parts[2 * p + 1], order) for p, order in enumerate(HALVING)
    ]

    attended_other = swap(attended[BLOCK:], "c")
    attended_out = join_heads(core, attended, attended_other)

    holds, finished = [], []
    for members, exchanged, last in GROUPS:
        holds.append(place_bit(last) == core)
        finished += finish_group([reduced[p] for p in members], exchanged, last)
    kept, sent = sort_pieces(jnp.stack(holds).astype(jnp.int32), finished)
    received = swap(sent, "c")
    new_weights, new_first, new_second = adam(
        core, kept, received, weights_master, adam_first, adam_second
    )
    return (attended_out, new_weights, new_first, new_second)


def solution(mesh):
    torus = Mesh(mesh.devices.reshape(4, 4, 4, 2), ("x", "y", "z", "c"))
    rows = P(("z", "c"), ("x", "y"), None)
    shard = P(("z", "c"), None)
    return jax.shard_map(
        step,
        mesh=torus,
        in_specs=(rows, shard, shard, shard, rows),
        out_specs=(rows, shard, shard, shard),
        check_vma=False,
    )
```

```python
import jax
import jax.numpy as jnp
from jax import lax
from jax.experimental import pallas as pl
from jax.experimental.pallas import tpu as pltpu
from jax.sharding import Mesh, PartitionSpec as P


HDIM = 128
BLOCK = 512
STEP = 100
HEADS_CORE = 4

EPS_NORM = 1e-05
BETA_ONE = 0.9
BETA_TWO = 0.95
LEARN_RATE = 0.001
DECAY_WEIGHT = 0.1
EPS_ADAM = 1e-08

BF = jnp.bfloat16
F32 = jnp.float32


PAIRS = {
    "0": [(0, 1), (1, 0), (2, 3), (3, 2)],
    "1": [(1, 2), (2, 1), (3, 0), (0, 3)],
}
CORE_SWAP = [(0, 1), (1, 0)]

GATHER_ORDERS = [("z0", "z1"), ("z1", "z0")]
HALVING = [
    ("z0", "x0", "z1"),
    ("z1", "y0", "z0"),
    ("x1", "z0", "z1"),
    ("y1", "z1", "z0"),
    ("z0", "x0", "z1"),
    ("z1", "y0", "z0"),
]
GROUPS = [
    ((0, 4), ("x1", "y1", "y0"), "x0"),
    ((1, 5), ("y1", "x1", "x0"), "y0"),
    ((2,), ("y0", "x0", "y1"), "x1"),
    ((3,), ("x0", "y0", "x1"), "y1"),
]
WIDTH = HEADS_CORE * HDIM
ROWS = 2 * BLOCK
VMEM = pl.BlockSpec(memory_space=pltpu.VMEM)
barrier = lax.optimization_barrier


def swap(x, dim):
    if dim == "c":
        return lax.ppermute(x, "c", CORE_SWAP)
    return lax.ppermute(x, dim[0], PAIRS[dim[1]])


def gray(place):
    return place ^ (place >> 1)


def place_bit(dim):
    code = gray(lax.axis_index(dim[0]))
    return (code >> int(dim[1])) & 1


def colour():
    return (lax.axis_index("x") + lax.axis_index("y")) & 1


def block_order():
    blocks = []
    for i in range(8):
        code = gray(lax.axis_index("z")) ^ (i >> 2) ^ (((i >> 1) & 1) << 1)
        blocks.append(2 * (code ^ (code >> 1)) + (colour() ^ (i & 1)))
    return jnp.stack(blocks).astype(jnp.int32)


def dot(a, b, ca, cb):
    return lax.dot_general(a, b, (((ca,), (cb,)), ((), ())), preferred_element_type=F32)


def causal(x):
    rows = lax.broadcasted_iota(jnp.int32, x.shape, 0)
    cols = lax.broadcasted_iota(jnp.int32, x.shape, 1)
    return jnp.where(rows >= cols, x, 0.0).astype(BF)


def shape(dims, dtype):
    return jax.ShapeDtypeStruct(dims, dtype)


def prepare_kernel(core, *refs):
    for out, parts in ((refs[7], refs[:3]), (refs[8], refs[3:6])):
        for t in range(HEADS_CORE):
            for u in range(3):
                kind, head = place_of(t, u)
                out[t, :, u * HDIM : (u + 1) * HDIM] = parts[kind][:, cols(head)].astype(BF)
    refs[9][...] = refs[6][...]


def place_of(chunk, slot):
    place = 3 * (chunk % 2) + slot
    return place // 2, 2 * (chunk // 2) + place % 2


def cols(h):
    return slice(h * HDIM, (h + 1) * HDIM)


def prepare(core, master, cot):
    def spec(j, other):
        def index(i, c):
            return i, 2 * j + (1 - c[0] if other else c[0])

        return pl.BlockSpec((128, WIDTH), index)

    out = pl.BlockSpec((HEADS_CORE, 128, 3 * HDIM), lambda i, c: (0, i, 0))
    return pl.pallas_call(
        prepare_kernel,
        name="prepare",
        grid_spec=pltpu.PrefetchScalarGridSpec(
            num_scalar_prefetch=1,
            grid=(2,),
            in_specs=[spec(j, other) for other in (False, True) for j in range(3)]
            + [pl.BlockSpec((256, WIDTH), lambda i, c: (i, 1 - c[0]))],
            out_specs=(out, out, pl.BlockSpec((256, WIDTH), lambda i, c: (i, 0))),
        ),
        out_shape=(shape((HEADS_CORE, 256, 3 * HDIM), BF),) * 2 + (shape((BLOCK, WIDTH), BF),),
    )(core.reshape(1), *([master] * 6), cot)


def arrange_kernel(blocks, own, other, out):
    out[:BLOCK, :] = own[...]
    out[BLOCK:, :] = other[...]


def arrange(blocks, own, other):
    tile = pl.BlockSpec((BLOCK, 256), lambda i, b: (0, b[i]))
    return pl.pallas_call(
        arrange_kernel,
        name="arrange",
        grid_spec=pltpu.PrefetchScalarGridSpec(
            num_scalar_prefetch=1,
            grid=(8,),
            in_specs=[tile, tile],
            out_specs=pl.BlockSpec((ROWS, 256), lambda i, b: (0, i)),
        ),
        out_shape=shape((ROWS, own.shape[1]), BF),
    )(blocks, own, other)


def outer_kernel(k0, v0, k1, v1, kv):
    for pair, (keys, values) in enumerate(((k0, v0), (k1, v1))):
        for h in range(2):
            kv[2 * pair + h, 0] = dot(keys[:, cols(h)], values[:, cols(h)], 0, 0)


def own_states(first, second):
    keys = pl.BlockSpec((BLOCK, 256), lambda s: (s, 1))
    values = pl.BlockSpec((BLOCK, 256), lambda s: (s, 2))
    return pl.pallas_call(
        outer_kernel,
        name="outer",
        grid=(2,),
        in_specs=[keys, values, keys, values],
        out_specs=pl.BlockSpec((HEADS_CORE, 1, HDIM, HDIM), lambda s: (0, s, 0, 0)),
        out_shape=shape((HEADS_CORE, 2, HDIM, HDIM), F32),
    )(first, first, second, second)


def project(tokens, pieces):
    chunks = []
    for h, order in enumerate(GATHER_ORDERS):
        mine, low, high = pieces[3 * h : 3 * h + 3]
        theirs = (low, high)
        rows = []
        for i in range(8):
            flips = {"z0": i >> 2, "z1": (i >> 1) & 1}
            place = flips[order[0]] + 2 * flips[order[1]]
            rows.append(theirs[place // 2][place % 2] if i & 1 else mine[place])
        chunks.append(jnp.concatenate(rows, 0))
    weights = jnp.concatenate(chunks, 1)
    return jnp.dot(tokens, weights, preferred_element_type=F32).astype(BF)


def lower_scores(a, b):
    low = dot(a[256:], b, 1, 1)
    return causal(dot(a[:256], b[:256], 1, 1)), low[:, :256].astype(BF), causal(low[:, 256:])


def times(scores, x):
    first, left, right = scores
    low = jnp.concatenate([left, right], 1)
    return jnp.concatenate([dot(first, x[:256], 1, 0), dot(low, x, 1, 0)], 0)


def turned_times(scores, x):
    first, left, right = scores
    column = jnp.concatenate([first, left], 0)
    return jnp.concatenate([dot(column, x, 0, 0), dot(right, x[256:], 0, 0)], 0)


def running_kernel(received, out):
    total = jnp.zeros(received.shape[1:], F32)
    for place in range(received.shape[0]):
        out[place] = total.astype(BF)
        total = total + received[place]


def earlier_states(kv):
    cut = kv.reshape(16, -1, HDIM)
    received = lax.all_to_all(cut, ("x", "y"), 0, 0, tiled=True)
    sums = pl.pallas_call(
        running_kernel,
        name="running",
        out_shape=shape(received.shape, BF),
        in_specs=[VMEM],
        out_specs=VMEM,
    )(received)
    return lax.all_to_all(sums, ("x", "y"), 0, 0, tiled=True).reshape(kv.shape)


def head_of(ref, h, kind):
    return ref[:, pl.ds(pl.multiple_of((2 * "qkv".index(kind) + h) * HDIM, HDIM), HDIM)]


def head_cols(h):
    return pl.ds(pl.multiple_of(h * HDIM, HDIM), HDIM)


def each_head(body):
    def one(h, carry):
        body(h)
        return carry

    lax.fori_loop(0, 2, one, 0)


def pair_specs():
    qkv_rows = (BLOCK, 6 * HDIM)
    return [
        pl.BlockSpec(qkv_rows, lambda p, s, *_: (jnp.where(p == 0, s, 1), 0)),
        pl.BlockSpec(qkv_rows, lambda p, s, *_: (jnp.where(p == 0, 0, s), 0)),
    ]


def head_rows():
    return pl.BlockSpec((BLOCK, 256), lambda p, s, *_: (s, p))


def pick(first, second, h, kinds):
    pair = pl.program_id(0)
    return [jnp.where(pair == 0, head_of(first, h, j), head_of(second, h, j)) for j in kinds]


def within_kernel(first, second, out):
    @each_head
    def _(h):
        q, k, v = pick(first, second, h, "qkv")
        out[:, head_cols(h)] = times(lower_scores(q, k), v)


def local_scores(first, second):
    return pl.pallas_call(
        within_kernel,
        name="within",
        grid=(2, 2),
        in_specs=pair_specs(),
        out_specs=head_rows(),
        out_shape=shape((ROWS, WIDTH), F32),
    )(first, second)


def forward_kernel(core, first, second, within, state, cot_own, cot_other, attended, grad, qg):
    s = pl.program_id(1)

    @each_head
    def _(h):
        (q,) = pick(first, second, h, "q")
        at = head_cols(h)
        mixed = within[:, at] + dot(q, state[h, 0], 1, 0)
        inverse = lax.rsqrt(jnp.mean(mixed * mixed, -1, keepdims=True) + EPS_NORM)
        normed = mixed * inverse
        attended[:, at] = normed.astype(BF)
        out_grad = jnp.where(s == 0, cot_own[:, at], cot_other[:, at]).astype(F32)
        along = jnp.mean(out_grad * normed, -1, keepdims=True)
        g = (inverse * (out_grad - normed * along)).astype(BF)
        grad[:, at] = g
        qg[h, 0] = dot(q, g, 0, 0).astype(BF)


def forward(core, first, second, within, state, cot_own, cot_other):
    rows = head_rows()
    states = pl.BlockSpec((2, 1, HDIM, HDIM), lambda p, s, c: (p, s, 0, 0))
    queries = (BLOCK, 2 * HDIM)
    return pl.pallas_call(
        forward_kernel,
        name="forward",
        grid_spec=pltpu.PrefetchScalarGridSpec(
            num_scalar_prefetch=1,
            grid=(2, 2),
            in_specs=[
                pl.BlockSpec(queries, lambda p, s, c: (jnp.where(p == 0, s, 1), 0)),
                pl.BlockSpec(queries, lambda p, s, c: (jnp.where(p == 0, 0, s), 0)),
                rows,
                states,
                pl.BlockSpec((BLOCK, 256), lambda p, s, c: (0, 2 * c[0] + p)),
                pl.BlockSpec((BLOCK, 256), lambda p, s, c: (0, p)),
            ],
            out_specs=(rows, rows, states),
        ),
        out_shape=(
            shape((ROWS, WIDTH), BF),
            shape((ROWS, WIDTH), BF),
            shape((HEADS_CORE, 2, HDIM, HDIM), BF),
        ),
    )(core.reshape(1), first, second, within, state, cot_own, cot_other)


def backward_kernel(pair, qkv, grad, state, dq, dkv):
    for h in range(2):
        q, k, v = [qkv[:, cols(2 * j + h)] for j in range(3)]
        at = cols(h)
        g = grad[:, at]
        back = lower_scores(g, v)
        dq[:, at] = (times(back, k) + dot(g, state[h, 0], 1, 1)).astype(BF)
        dkv[0, :, at] = turned_times(back, q)
        dkv[1, :, at] = turned_times(lower_scores(q, k), g)


def backward(pair, qkv, grad, state):
    return pl.pallas_call(
        backward_kernel,
        name="backward",
        grid_spec=pltpu.PrefetchScalarGridSpec(
            num_scalar_prefetch=1,
            grid=(2,),
            in_specs=[
                pl.BlockSpec((BLOCK, 6 * HDIM), lambda s, p: (s, 0)),
                pl.BlockSpec((BLOCK, 256), lambda s, p: (s, p[0])),
                pl.BlockSpec((2, 1, HDIM, HDIM), lambda s, p: (p[0], s, 0, 0)),
            ],
            out_specs=(
                pl.BlockSpec((BLOCK, 256), lambda s, p: (s, 0)),
                pl.BlockSpec((2, BLOCK, 256), lambda s, p: (0, s, 0)),
            ),
        ),
        out_shape=(shape((ROWS, 256), BF), shape((2, ROWS, 256), F32)),
    )(jnp.full((1,), pair, jnp.int32), qkv, grad, state)


def token_copy(i, tokens, held, sems):
    at = pl.ds(pl.multiple_of(i * 512, 512), 512)
    return pltpu.make_async_copy(tokens.at[:, at], held.at[:, at], sems.at[i])


def fetch_tokens(tokens, held, sems):
    for i in range(4):
        token_copy(i, tokens, held, sems).start()


def multiply_blocks(first, keeps, turned, held, arriving, outs):
    def blocks(i, carry):
        if arriving is not None:
            token_copy(i, *arriving).wait()
        at = pl.ds(pl.multiple_of(i * 512, 512), 512)
        piece = dot(turned[...], held[:, at], 1, 0).astype(BF)
        for part in range(2):
            sent, kept = outs[2 * part], outs[2 * part + 1]
            even = piece[part * 256 : (part + 1) * 256, :256]
            odd = piece[part * 256 : (part + 1) * 256, 256:]
            dim = HALVING[first + part][0]
            if dim[0] != "z":
                straight = keeps[part] == 0
                kept[i] = jnp.where(straight, even, odd)
                sent[i] = jnp.where(straight, odd, even)
                continue
            bits = (i >> 1, i & 1)
            moves, place = bits[int(dim[1])], 2 * bits[1 - int(dim[1])]

            @pl.when(moves == 1)
            def _():
                sent[place] = even
                sent[place + 1] = odd

            @pl.when(moves == 0)
            def _():
                kept[place] = even
                kept[place + 1] = odd

        return carry

    lax.fori_loop(0, 4, blocks, 0)


def query_gradient_kernel(keeps, q0, q1, tokens, s0, k0, s1, k1, turned, held, sems):
    fetch_tokens(tokens, held, sems)
    turned[:256, :] = q0[...].T
    turned[256:, :] = q1[...].T
    multiply_blocks(0, keeps, turned, held, (tokens, held, sems), (s0, k0, s1, k1))


def gradient_kernel(keeps, k0, v0, k1, v1, d0, d1, state, tokens, *refs):
    outs, (turned, held, sems) = refs[:8], refs[8:]
    fetch_tokens(tokens, held, sems)
    for kind in range(2):
        sides = ((v0 if kind == 0 else k0, d0), (v1 if kind == 0 else k1, d1))
        for pair, (source, within) in enumerate(sides):

            @each_head
            def _(h):
                head = 2 * pair + h
                at = head_cols(h)
                for s in range(2):
                    span = slice(s * BLOCK, (s + 1) * BLOCK)
                    later = dot(source[span, at], state[head, s], 1, 1 - kind)
                    total = within[kind, span, at] + later
                    turned[head_cols(head), span] = total.astype(BF).T

        arriving = (tokens, held, sems) if kind == 0 else None
        multiply_blocks(2 + 2 * kind, keeps, turned, held, arriving, outs[4 * kind : 4 * kind + 4])


def gradient_call(kernel, first, ins, specs, tokens):
    count = len(first)
    keeps = jnp.stack([colour() ^ place_bit(HALVING[p][0]) for p in (2, 3)]).astype(jnp.int32)
    return pl.pallas_call(
        kernel,
        grid=(1,),
        in_specs=[pl.BlockSpec(memory_space=pltpu.SMEM)]
        + specs
        + [pl.BlockSpec(memory_space=pl.ANY)],
        out_specs=(VMEM,) * (2 * count),
        out_shape=(shape((4, 256, 256), BF),) * (2 * count),
        scratch_shapes=[
            pltpu.VMEM((WIDTH, ROWS), BF),
            pltpu.VMEM((ROWS, 2048), BF),
            pltpu.SemaphoreType.DMA((4,)),
        ],
    )(keeps, *ins, tokens)


def query_gradient(q0, q1, tokens):
    return gradient_call(query_gradient_kernel, (0, 1), (q0, q1), [VMEM] * 2, tokens)


def key_value_gradient(first, second, d_first, d_second, state, tokens):
    specs = [pl.BlockSpec((ROWS, 256), lambda _, j=j: (0, j)) for j in (1, 2)] * 2 + [VMEM] * 3
    ins = (first, first, second, second, d_first, d_second, state)
    return gradient_call(gradient_kernel, (2, 3, 4, 5), ins, specs, tokens)


def wide(x):
    return x.astype(F32)


def add(a, b):
    return (wide(a) + wide(b)).astype(BF)


def reduce_part(sent, kept, order):
    received = swap(sent, order[0])
    part = add(kept, received).reshape(2, 2, 256, 256)
    if order[0][0] == "z":
        keeps = colour() ^ place_bit(order[1])
        send = lax.dynamic_index_in_dim(part, 1 - keeps, 1, False)
        keep = lax.dynamic_index_in_dim(part, keeps, 1, False)
    else:
        send = lax.index_in_dim(part, 1, int(order[1][1]), False)
        keep = lax.index_in_dim(part, 0, int(order[1][1]), False)
    part = add(keep, swap(send, order[1]))
    return add(part[0], swap(part[1], order[2]))


def finish_group(parts, exchanged, last):
    total = jnp.stack(parts)
    for dim in exchanged:
        total = add(total, swap(total, dim))
    return total, swap(total, last)


def later_steps(total, later):
    total = wide(total)
    carried = jnp.zeros_like(total)
    for dim in ("y0", "y1", "x0", "x1"):
        moving = swap(total.astype(BF), dim)
        received = yield moving
        received = wide(received)
        upper = (lax.axis_index(dim[0]) >> int(dim[1])) & 1
        carried = carried + jnp.where(upper == (0 if later else 1), received, 0.0)
        total = total + received
    yield carried.astype(BF)


def sort_kernel(holds, *refs):
    kept, sent = refs[-2:]
    for g, (members, _, _) in enumerate(GROUPS):
        straight = holds[g] == 1
        for j, p in enumerate(members):
            at = slice(p * 256, (p + 1) * 256)
            here, there = refs[2 * g][j], refs[2 * g + 1][j]
            kept[:, at] = jnp.where(straight, here, there).T
            sent[:, at] = jnp.where(straight, there, here).T


def sort_pieces(holds, finished):
    return pl.pallas_call(
        sort_kernel,
        name="sort_pieces",
        in_specs=[pl.BlockSpec(memory_space=pltpu.SMEM)] + [VMEM] * len(finished),
        out_specs=(VMEM, VMEM),
        out_shape=(shape((256, 3 * WIDTH), BF),) * 2,
    )(holds, *finished)


def join_kernel(core, own, other, out):
    straight = core[0] == 0
    out[0, :, :WIDTH] = jnp.where(straight, own[...], other[...])
    out[0, :, WIDTH:] = jnp.where(straight, other[...], own[...])


def join_heads(core, own, other):
    half = pl.BlockSpec((256, WIDTH), lambda i, c: (i, 0))
    return pl.pallas_call(
        join_kernel,
        name="join_heads",
        grid_spec=pltpu.PrefetchScalarGridSpec(
            num_scalar_prefetch=1,
            grid=(2,),
            in_specs=[half, half],
            out_specs=pl.BlockSpec((1, 256, 2 * WIDTH), lambda i, c: (0, i, 0)),
        ),
        out_shape=shape((1, BLOCK, 2 * WIDTH), BF),
    )(core.reshape(1), own, other)


def assemble_kernel(core, kept, received, out):
    for block in range(6):
        source = slice((block // 2) * WIDTH, (block // 2 + 1) * WIDTH)
        straight = core[0] == block % 2
        out[:, block * WIDTH : (block + 1) * WIDTH] = jnp.where(
            straight, kept[:, source], received[:, source]
        )


def assemble(core, kept, received):
    return pl.pallas_call(
        assemble_kernel,
        name="assemble",
        in_specs=[pl.BlockSpec(memory_space=pltpu.SMEM), VMEM, VMEM],
        out_specs=VMEM,
        out_shape=shape((256, 6 * WIDTH), BF),
    )(core.reshape(1), kept, received)


def adam(core, kept, received, weights, first, second):
    gradient = assemble(core, kept, received).astype(F32)
    new_first = BETA_ONE * first + (1.0 - BETA_ONE) * gradient
    new_second = BETA_TWO * second + (1.0 - BETA_TWO) * gradient * gradient
    first_hat = new_first * (1.0 / (1.0 - BETA_ONE**STEP))
    second_hat = new_second * (1.0 / (1.0 - BETA_TWO**STEP))
    new_weights = weights - LEARN_RATE * (
        first_hat / (jnp.sqrt(second_hat) + EPS_ADAM) + DECAY_WEIGHT * weights
    )
    return new_weights, new_first, new_second


def gather_step(step, mine):
    got = []
    for h in range(2):
        got.append(swap(mine[h], GATHER_ORDERS[h][step]))
    return [jnp.concatenate([mine[h], got[h]], 0) for h in range(2)]


def exchange_colours(mine):
    pieces = []
    for h, axis in enumerate("xy"):
        pieces.append(mine[h])
        for side in range(2):
            pieces.append(swap(mine[h][2 * side : 2 * side + 2], f"{axis}{side}"))
    return pieces


def step(tokens, weights_master, adam_first, adam_second, cotangent):
    core = lax.axis_index("c")
    own = tokens[0]
    straight = colour() == core

    held, outgoing, cot_out = prepare(core, weights_master, cotangent[0])
    traded = swap(outgoing, "c")
    other = swap(own, "c")
    cot_other = swap(cot_out, "c")

    blocks = block_order()
    mine = jnp.where(straight, held, traded)
    first = gather_step(0, [mine[0][None], mine[1][None]])
    first = gather_step(1, first)
    both = arrange(blocks, own, other)
    first, mine, both = barrier((first, mine, both))
    pieces = exchange_colours(first)
    second = gather_step(0, [mine[2][None], mine[3][None]])
    second = gather_step(1, second)
    qkv_first = project(both, pieces)
    second, qkv_first = barrier((second, qkv_first))
    qkv_second = project(both, exchange_colours(second))

    state = earlier_states(own_states(qkv_first, qkv_second))
    within = local_scores(qkv_first, qkv_second)
    attended, grad, qg = forward(
        core, qkv_first, qkv_second, within, state, cotangent[0], cot_other
    )

    steps = later_steps(qg, True)
    received = next(steps)
    q0, d0 = backward(0, qkv_first, grad, state)
    received, q0, d0, grad = barrier((received, q0, d0, grad))
    received = steps.send(received)
    q1, d1 = backward(1, qkv_second, grad, state)
    received, q0, q1, d1 = barrier((received, q0, q1, d1))
    received = steps.send(received)
    parts = query_gradient(q0, q1, both)
    received, parts = barrier((received, parts))
    received = steps.send(received)
    later = steps.send(received)
    parts += key_value_gradient(qkv_first, qkv_second, d0, d1, later, both)
    reduced = [
        reduce_part(parts[2 * p], parts[2 * p + 1], order) for p, order in enumerate(HALVING)
    ]

    attended_other = swap(attended[BLOCK:], "c")
    attended_out = join_heads(core, attended, attended_other)

    holds, finished = [], []
    for members, exchanged, last in GROUPS:
        holds.append(place_bit(last) == core)
        finished += finish_group([reduced[p] for p in members], exchanged, last)
    kept, sent = sort_pieces(jnp.stack(holds).astype(jnp.int32), finished)
    received = swap(sent, "c")
    new_weights, new_first, new_second = adam(
        core, kept, received, weights_master, adam_first, adam_second
    )
    return (attended_out, new_weights, new_first, new_second)


def solution(mesh):
    torus = Mesh(mesh.devices.reshape(4, 4, 4, 2), ("x", "y", "z", "c"))
    rows = P(("z", "c"), ("x", "y"), None)
    shard = P(("z", "c"), None)
    return jax.shard_map(
        step,
        mesh=torus,
        in_specs=(rows, shard, shard, shard, rows),
        out_specs=(rows, shard, shard, shard),
        check_vma=False,
    )
```

```python
import jax
import jax.numpy as jnp
from jax import lax
from jax.experimental import pallas as pl
from jax.experimental.pallas import tpu as pltpu
from jax.sharding import Mesh, PartitionSpec as P


HDIM = 128
BLOCK = 512
STEP = 100
HEADS_CORE = 4

EPS_NORM = 1e-05
BETA_ONE = 0.9
BETA_TWO = 0.95
LEARN_RATE = 0.001
DECAY_WEIGHT = 0.1
EPS_ADAM = 1e-08

BF = jnp.bfloat16
F32 = jnp.float32


PAIRS = {
    "0": [(0, 1), (1, 0), (2, 3), (3, 2)],
    "1": [(1, 2), (2, 1), (3, 0), (0, 3)],
}
CORE_SWAP = [(0, 1), (1, 0)]

GATHER_ORDERS = [("z0", "z1"), ("z1", "z0")]
HALVING = [
    ("z0", "x0", "z1"),
    ("z1", "y0", "z0"),
    ("x1", "z0", "z1"),
    ("y1", "z1", "z0"),
    ("z0", "x0", "z1"),
    ("z1", "y0", "z0"),
]
GROUPS = [
    ((0, 4), ("x1", "y1", "y0"), "x0"),
    ((1, 5), ("y1", "x1", "x0"), "y0"),
    ((2,), ("y0", "x0", "y1"), "x1"),
    ((3,), ("x0", "y0", "x1"), "y1"),
]
WIDTH = HEADS_CORE * HDIM
ROWS = 2 * BLOCK
VMEM = pl.BlockSpec(memory_space=pltpu.VMEM)
barrier = lax.optimization_barrier


def swap(x, dim):
    if dim == "c":
        return lax.ppermute(x, "c", CORE_SWAP)
    return lax.ppermute(x, dim[0], PAIRS[dim[1]])


def gray(place):
    return place ^ (place >> 1)


def place_bit(dim):
    code = gray(lax.axis_index(dim[0]))
    return (code >> int(dim[1])) & 1


def colour():
    return (lax.axis_index("x") + lax.axis_index("y")) & 1


def block_order():
    blocks = []
    for i in range(8):
        code = gray(lax.axis_index("z")) ^ (i >> 2) ^ (((i >> 1) & 1) << 1)
        blocks.append(2 * (code ^ (code >> 1)) + (colour() ^ (i & 1)))
    return jnp.stack(blocks).astype(jnp.int32)


def dot(a, b, ca, cb):
    return lax.dot_general(a, b, (((ca,), (cb,)), ((), ())), preferred_element_type=F32)


def causal(x):
    rows = lax.broadcasted_iota(jnp.int32, x.shape, 0)
    cols = lax.broadcasted_iota(jnp.int32, x.shape, 1)
    return jnp.where(rows >= cols, x, 0.0).astype(BF)


def shape(dims, dtype):
    return jax.ShapeDtypeStruct(dims, dtype)


def prepare_kernel(core, *refs):
    for out, parts in ((refs[7], refs[:3]), (refs[8], refs[3:6])):
        for t in range(HEADS_CORE):
            for u in range(3):
                kind, head = place_of(t, u)
                out[t, :, u * HDIM : (u + 1) * HDIM] = parts[kind][:, cols(head)].astype(BF)
    refs[9][...] = refs[6][...]


def place_of(chunk, slot):
    place = 3 * (chunk % 2) + slot
    return place // 2, 2 * (chunk // 2) + place % 2


def cols(h):
    return slice(h * HDIM, (h + 1) * HDIM)


def prepare(core, master, cot):
    def spec(j, other):
        def index(i, c):
            return i, 2 * j + (1 - c[0] if other else c[0])

        return pl.BlockSpec((128, WIDTH), index)

    out = pl.BlockSpec((HEADS_CORE, 128, 3 * HDIM), lambda i, c: (0, i, 0))
    return pl.pallas_call(
        prepare_kernel,
        name="prepare",
        grid_spec=pltpu.PrefetchScalarGridSpec(
            num_scalar_prefetch=1,
            grid=(2,),
            in_specs=[spec(j, other) for other in (False, True) for j in range(3)]
            + [pl.BlockSpec((256, WIDTH), lambda i, c: (i, 1 - c[0]))],
            out_specs=(out, out, pl.BlockSpec((256, WIDTH), lambda i, c: (i, 0))),
        ),
        out_shape=(shape((HEADS_CORE, 256, 3 * HDIM), BF),) * 2 + (shape((BLOCK, WIDTH), BF),),
    )(core.reshape(1), *([master] * 6), cot)


def arrange_kernel(blocks, own, other, out):
    out[:BLOCK, :] = own[...]
    out[BLOCK:, :] = other[...]


def arrange(blocks, own, other):
    tile = pl.BlockSpec((BLOCK, 256), lambda i, b: (0, b[i]))
    return pl.pallas_call(
        arrange_kernel,
        name="arrange",
        grid_spec=pltpu.PrefetchScalarGridSpec(
            num_scalar_prefetch=1,
            grid=(8,),
            in_specs=[tile, tile],
            out_specs=pl.BlockSpec((ROWS, 256), lambda i, b: (0, i)),
        ),
        out_shape=shape((ROWS, own.shape[1]), BF),
    )(blocks, own, other)


def outer_kernel(k0, v0, k1, v1, kv):
    for pair, (keys, values) in enumerate(((k0, v0), (k1, v1))):
        for h in range(2):
            kv[2 * pair + h, 0] = dot(keys[:, cols(h)], values[:, cols(h)], 0, 0)


def own_states(first, second):
    keys = pl.BlockSpec((BLOCK, 256), lambda s: (s, 1))
    values = pl.BlockSpec((BLOCK, 256), lambda s: (s, 2))
    return pl.pallas_call(
        outer_kernel,
        name="outer",
        grid=(2,),
        in_specs=[keys, values, keys, values],
        out_specs=pl.BlockSpec((HEADS_CORE, 1, HDIM, HDIM), lambda s: (0, s, 0, 0)),
        out_shape=shape((HEADS_CORE, 2, HDIM, HDIM), F32),
    )(first, first, second, second)


def project(tokens, pieces):
    chunks = []
    for h, order in enumerate(GATHER_ORDERS):
        mine, low, high = pieces[3 * h : 3 * h + 3]
        theirs = (low, high)
        rows = []
        for i in range(8):
            flips = {"z0": i >> 2, "z1": (i >> 1) & 1}
            place = flips[order[0]] + 2 * flips[order[1]]
            rows.append(theirs[place // 2][place % 2] if i & 1 else mine[place])
        chunks.append(jnp.concatenate(rows, 0))
    weights = jnp.concatenate(chunks, 1)
    return jnp.dot(tokens, weights, preferred_element_type=F32).astype(BF)


def lower_scores(a, b):
    low = dot(a[256:], b, 1, 1)
    return causal(dot(a[:256], b[:256], 1, 1)), low[:, :256].astype(BF), causal(low[:, 256:])


def times(scores, x):
    first, left, right = scores
    low = jnp.concatenate([left, right], 1)
    return jnp.concatenate([dot(first, x[:256], 1, 0), dot(low, x, 1, 0)], 0)


def turned_times(scores, x):
    first, left, right = scores
    column = jnp.concatenate([first, left], 0)
    return jnp.concatenate([dot(column, x, 0, 0), dot(right, x[256:], 0, 0)], 0)


def running_kernel(received, out):
    total = jnp.zeros(received.shape[1:], F32)
    for place in range(received.shape[0]):
        out[place] = total.astype(BF)
        total = total + received[place]


def earlier_states(kv):
    cut = kv.reshape(16, -1, HDIM)
    received = lax.all_to_all(cut, ("x", "y"), 0, 0, tiled=True)
    sums = pl.pallas_call(
        running_kernel,
        name="running",
        out_shape=shape(received.shape, BF),
        in_specs=[VMEM],
        out_specs=VMEM,
    )(received)
    return lax.all_to_all(sums, ("x", "y"), 0, 0, tiled=True).reshape(kv.shape)


def head_of(ref, h, kind):
    return ref[:, pl.ds(pl.multiple_of((2 * "qkv".index(kind) + h) * HDIM, HDIM), HDIM)]


def head_cols(h):
    return pl.ds(pl.multiple_of(h * HDIM, HDIM), HDIM)


def each_head(body):
    def one(h, carry):
        body(h)
        return carry

    lax.fori_loop(0, 2, one, 0)


def pair_specs():
    qkv_rows = (BLOCK, 6 * HDIM)
    return [
        pl.BlockSpec(qkv_rows, lambda p, s, *_: (jnp.where(p == 0, s, 1), 0)),
        pl.BlockSpec(qkv_rows, lambda p, s, *_: (jnp.where(p == 0, 0, s), 0)),
    ]


def head_rows():
    return pl.BlockSpec((BLOCK, 256), lambda p, s, *_: (s, p))


def pick(first, second, h, kinds):
    pair = pl.program_id(0)
    return [jnp.where(pair == 0, head_of(first, h, j), head_of(second, h, j)) for j in kinds]


def within_kernel(first, second, out):
    @each_head
    def _(h):
        q, k, v = pick(first, second, h, "qkv")
        out[:, head_cols(h)] = times(lower_scores(q, k), v)


def local_scores(first, second):
    return pl.pallas_call(
        within_kernel,
        name="within",
        grid=(2, 2),
        in_specs=pair_specs(),
        out_specs=head_rows(),
        out_shape=shape((ROWS, WIDTH), F32),
    )(first, second)


def forward_kernel(core, first, second, within, state, cot_own, cot_other, attended, grad, qg):
    s = pl.program_id(1)

    @each_head
    def _(h):
        (q,) = pick(first, second, h, "q")
        at = head_cols(h)
        mixed = within[:, at] + dot(q, state[h, 0], 1, 0)
        inverse = lax.rsqrt(jnp.mean(mixed * mixed, -1, keepdims=True) + EPS_NORM)
        normed = mixed * inverse
        attended[:, at] = normed.astype(BF)
        out_grad = jnp.where(s == 0, cot_own[:, at], cot_other[:, at]).astype(F32)
        along = jnp.mean(out_grad * normed, -1, keepdims=True)
        g = (inverse * (out_grad - normed * along)).astype(BF)
        grad[:, at] = g
        qg[h, 0] = dot(q, g, 0, 0).astype(BF)


def forward(core, first, second, within, state, cot_own, cot_other):
    rows = head_rows()
    states = pl.BlockSpec((2, 1, HDIM, HDIM), lambda p, s, c: (p, s, 0, 0))
    queries = (BLOCK, 2 * HDIM)
    return pl.pallas_call(
        forward_kernel,
        name="forward",
        grid_spec=pltpu.PrefetchScalarGridSpec(
            num_scalar_prefetch=1,
            grid=(2, 2),
            in_specs=[
                pl.BlockSpec(queries, lambda p, s, c: (jnp.where(p == 0, s, 1), 0)),
                pl.BlockSpec(queries, lambda p, s, c: (jnp.where(p == 0, 0, s), 0)),
                rows,
                states,
                pl.BlockSpec((BLOCK, 256), lambda p, s, c: (0, 2 * c[0] + p)),
                pl.BlockSpec((BLOCK, 256), lambda p, s, c: (0, p)),
            ],
            out_specs=(rows, rows, states),
        ),
        out_shape=(
            shape((ROWS, WIDTH), BF),
            shape((ROWS, WIDTH), BF),
            shape((HEADS_CORE, 2, HDIM, HDIM), BF),
        ),
    )(core.reshape(1), first, second, within, state, cot_own, cot_other)


def backward_kernel(pair, qkv, grad, state, dq, dkv):
    for h in range(2):
        q, k, v = [qkv[:, cols(2 * j + h)] for j in range(3)]
        at = cols(h)
        g = grad[:, at]
        back = lower_scores(g, v)
        dq[:, at] = (times(back, k) + dot(g, state[h, 0], 1, 1)).astype(BF)
        dkv[0, :, at] = turned_times(back, q)
        dkv[1, :, at] = turned_times(lower_scores(q, k), g)


def backward(pair, qkv, grad, state):
    return pl.pallas_call(
        backward_kernel,
        name="backward",
        grid_spec=pltpu.PrefetchScalarGridSpec(
            num_scalar_prefetch=1,
            grid=(2,),
            in_specs=[
                pl.BlockSpec((BLOCK, 6 * HDIM), lambda s, p: (s, 0)),
                pl.BlockSpec((BLOCK, 256), lambda s, p: (s, p[0])),
                pl.BlockSpec((2, 1, HDIM, HDIM), lambda s, p: (p[0], s, 0, 0)),
            ],
            out_specs=(
                pl.BlockSpec((BLOCK, 256), lambda s, p: (s, 0)),
                pl.BlockSpec((2, BLOCK, 256), lambda s, p: (0, s, 0)),
            ),
        ),
        out_shape=(shape((ROWS, 256), BF), shape((2, ROWS, 256), F32)),
    )(jnp.full((1,), pair, jnp.int32), qkv, grad, state)


def token_copy(i, tokens, held, sems):
    at = pl.ds(pl.multiple_of(i * 512, 512), 512)
    return pltpu.make_async_copy(tokens.at[:, at], held.at[:, at], sems.at[i])


def fetch_tokens(tokens, held, sems):
    for i in range(4):
        token_copy(i, tokens, held, sems).start()


def multiply_blocks(first, keeps, turned, held, arriving, outs):
    def blocks(i, carry):
        if arriving is not None:
            token_copy(i, *arriving).wait()
        at = pl.ds(pl.multiple_of(i * 512, 512), 512)
        piece = dot(turned[...], held[:, at], 1, 0).astype(BF)
        for part in range(2):
            sent, kept = outs[2 * part], outs[2 * part + 1]
            even = piece[part * 256 : (part + 1) * 256, :256]
            odd = piece[part * 256 : (part + 1) * 256, 256:]
            dim = HALVING[first + part][0]
            if dim[0] != "z":
                straight = keeps[part] == 0
                kept[i] = jnp.where(straight, even, odd)
                sent[i] = jnp.where(straight, odd, even)
                continue
            bits = (i >> 1, i & 1)
            moves, place = bits[int(dim[1])], 2 * bits[1 - int(dim[1])]

            @pl.when(moves == 1)
            def _():
                sent[place] = even
                sent[place + 1] = odd

            @pl.when(moves == 0)
            def _():
                kept[place] = even
                kept[place + 1] = odd

        return carry

    lax.fori_loop(0, 4, blocks, 0)


def query_gradient_kernel(keeps, q0, q1, tokens, s0, k0, s1, k1, turned, held, sems):
    fetch_tokens(tokens, held, sems)
    turned[:256, :] = q0[...].T
    turned[256:, :] = q1[...].T
    multiply_blocks(0, keeps, turned, held, (tokens, held, sems), (s0, k0, s1, k1))


def gradient_kernel(keeps, k0, v0, k1, v1, d0, d1, state, tokens, *refs):
    outs, (turned, held, sems) = refs[:8], refs[8:]
    fetch_tokens(tokens, held, sems)
    for kind in range(2):
        sides = ((v0 if kind == 0 else k0, d0), (v1 if kind == 0 else k1, d1))
        for pair, (source, within) in enumerate(sides):

            @each_head
            def _(h):
                head = 2 * pair + h
                at = head_cols(h)
                for s in range(2):
                    span = slice(s * BLOCK, (s + 1) * BLOCK)
                    later = dot(source[span, at], state[head, s], 1, 1 - kind)
                    total = within[kind, span, at] + later
                    turned[head_cols(head), span] = total.astype(BF).T

        arriving = (tokens, held, sems) if kind == 0 else None
        multiply_blocks(2 + 2 * kind, keeps, turned, held, arriving, outs[4 * kind : 4 * kind + 4])


def gradient_call(kernel, first, ins, specs, tokens):
    count = len(first)
    keeps = jnp.stack([colour() ^ place_bit(HALVING[p][0]) for p in (2, 3)]).astype(jnp.int32)
    return pl.pallas_call(
        kernel,
        grid=(1,),
        in_specs=[pl.BlockSpec(memory_space=pltpu.SMEM)]
        + specs
        + [pl.BlockSpec(memory_space=pl.ANY)],
        out_specs=(VMEM,) * (2 * count),
        out_shape=(shape((4, 256, 256), BF),) * (2 * count),
        scratch_shapes=[
            pltpu.VMEM((WIDTH, ROWS), BF),
            pltpu.VMEM((ROWS, 2048), BF),
            pltpu.SemaphoreType.DMA((4,)),
        ],
    )(keeps, *ins, tokens)


def query_gradient(q0, q1, tokens):
    return gradient_call(query_gradient_kernel, (0, 1), (q0, q1), [VMEM] * 2, tokens)


def key_value_gradient(first, second, d_first, d_second, state, tokens):
    specs = [pl.BlockSpec((ROWS, 256), lambda _, j=j: (0, j)) for j in (1, 2)] * 2 + [VMEM] * 3
    ins = (first, first, second, second, d_first, d_second, state)
    return gradient_call(gradient_kernel, (2, 3, 4, 5), ins, specs, tokens)


def wide(x):
    return x.astype(F32)


def add(a, b):
    return (wide(a) + wide(b)).astype(BF)


def reduce_part(sent, kept, order):
    received = swap(sent, order[0])
    part = add(kept, received).reshape(2, 2, 256, 256)
    if order[0][0] == "z":
        keeps = colour() ^ place_bit(order[1])
        send = lax.dynamic_index_in_dim(part, 1 - keeps, 1, False)
        keep = lax.dynamic_index_in_dim(part, keeps, 1, False)
    else:
        send = lax.index_in_dim(part, 1, int(order[1][1]), False)
        keep = lax.index_in_dim(part, 0, int(order[1][1]), False)
    part = add(keep, swap(send, order[1]))
    return add(part[0], swap(part[1], order[2]))


def finish_group(parts, exchanged, last):
    total = jnp.stack(parts)
    for dim in exchanged:
        total = add(total, swap(total, dim))
    return total, swap(total, last)


def later_steps(total, later):
    total = wide(total)
    carried = jnp.zeros_like(total)
    for dim in ("y0", "y1", "x0", "x1"):
        moving = swap(total.astype(BF), dim)
        received = yield moving
        received = wide(received)
        upper = (lax.axis_index(dim[0]) >> int(dim[1])) & 1
        carried = carried + jnp.where(upper == (0 if later else 1), received, 0.0)
        total = total + received
    yield carried.astype(BF)


def sort_kernel(holds, *refs):
    kept, sent = refs[-2:]
    for g, (members, _, _) in enumerate(GROUPS):
        straight = holds[g] == 1
        for j, p in enumerate(members):
            at = slice(p * 256, (p + 1) * 256)
            here, there = refs[2 * g][j], refs[2 * g + 1][j]
            kept[:, at] = jnp.where(straight, here, there).T
            sent[:, at] = jnp.where(straight, there, here).T


def sort_pieces(holds, finished):
    return pl.pallas_call(
        sort_kernel,
        name="sort_pieces",
        in_specs=[pl.BlockSpec(memory_space=pltpu.SMEM)] + [VMEM] * len(finished),
        out_specs=(VMEM, VMEM),
        out_shape=(shape((256, 3 * WIDTH), BF),) * 2,
    )(holds, *finished)


def join_kernel(core, own, other, out):
    straight = core[0] == 0
    out[0, :, :WIDTH] = jnp.where(straight, own[...], other[...])
    out[0, :, WIDTH:] = jnp.where(straight, other[...], own[...])


def join_heads(core, own, other):
    half = pl.BlockSpec((256, WIDTH), lambda i, c: (i, 0))
    return pl.pallas_call(
        join_kernel,
        name="join_heads",
        grid_spec=pltpu.PrefetchScalarGridSpec(
            num_scalar_prefetch=1,
            grid=(2,),
            in_specs=[half, half],
            out_specs=pl.BlockSpec((1, 256, 2 * WIDTH), lambda i, c: (0, i, 0)),
        ),
        out_shape=shape((1, BLOCK, 2 * WIDTH), BF),
    )(core.reshape(1), own, other)


def assemble_kernel(core, kept, received, out):
    for block in range(6):
        source = slice((block // 2) * WIDTH, (block // 2 + 1) * WIDTH)
        straight = core[0] == block % 2
        out[:, block * WIDTH : (block + 1) * WIDTH] = jnp.where(
            straight, kept[:, source], received[:, source]
        )


def assemble(core, kept, received):
    return pl.pallas_call(
        assemble_kernel,
        name="assemble",
        grid=(4,),
        in_specs=[pl.BlockSpec(memory_space=pltpu.SMEM)]
        + [pl.BlockSpec((64, 3 * WIDTH), lambda i: (i, 0))] * 2,
        out_specs=pl.BlockSpec((64, 6 * WIDTH), lambda i: (i, 0)),
        out_shape=shape((256, 6 * WIDTH), BF),
    )(core.reshape(1), kept, received)


def adam(core, kept, received, weights, first, second):
    gradient = assemble(core, kept, received).astype(F32)
    new_first = BETA_ONE * first + (1.0 - BETA_ONE) * gradient
    new_second = BETA_TWO * second + (1.0 - BETA_TWO) * gradient * gradient
    first_hat = new_first * (1.0 / (1.0 - BETA_ONE**STEP))
    second_hat = new_second * (1.0 / (1.0 - BETA_TWO**STEP))
    new_weights = weights - LEARN_RATE * (
        first_hat / (jnp.sqrt(second_hat) + EPS_ADAM) + DECAY_WEIGHT * weights
    )
    return new_weights, new_first, new_second


def gather_step(step, mine):
    got = []
    for h in range(2):
        got.append(swap(mine[h], GATHER_ORDERS[h][step]))
    return [jnp.concatenate([mine[h], got[h]], 0) for h in range(2)]


def exchange_colours(mine):
    pieces = []
    for h, axis in enumerate("xy"):
        pieces.append(mine[h])
        for side in range(2):
            pieces.append(swap(mine[h][2 * side : 2 * side + 2], f"{axis}{side}"))
    return pieces


def step(tokens, weights_master, adam_first, adam_second, cotangent):
    core = lax.axis_index("c")
    own = tokens[0]
    straight = colour() == core

    held, outgoing, cot_out = prepare(core, weights_master, cotangent[0])
    traded = swap(outgoing, "c")
    other = swap(own, "c")
    cot_other = swap(cot_out, "c")

    blocks = block_order()
    mine = jnp.where(straight, held, traded)
    first = gather_step(0, [mine[0][None], mine[1][None]])
    first = gather_step(1, first)
    both = arrange(blocks, own, other)
    first, mine, both = barrier((first, mine, both))
    pieces = exchange_colours(first)
    second = gather_step(0, [mine[2][None], mine[3][None]])
    second = gather_step(1, second)
    qkv_first = project(both, pieces)
    second, qkv_first = barrier((second, qkv_first))
    qkv_second = project(both, exchange_colours(second))

    state = earlier_states(own_states(qkv_first, qkv_second))
    within = local_scores(qkv_first, qkv_second)
    attended, grad, qg = forward(
        core, qkv_first, qkv_second, within, state, cotangent[0], cot_other
    )

    steps = later_steps(qg, True)
    received = next(steps)
    q0, d0 = backward(0, qkv_first, grad, state)
    received, q0, d0, grad = barrier((received, q0, d0, grad))
    received = steps.send(received)
    q1, d1 = backward(1, qkv_second, grad, state)
    received, q0, q1, d1 = barrier((received, q0, q1, d1))
    received = steps.send(received)
    parts = query_gradient(q0, q1, both)
    received, parts = barrier((received, parts))
    received = steps.send(received)
    later = steps.send(received)
    parts += key_value_gradient(qkv_first, qkv_second, d0, d1, later, both)
    reduced = [
        reduce_part(parts[2 * p], parts[2 * p + 1], order) for p, order in enumerate(HALVING)
    ]

    attended_other = swap(attended[BLOCK:], "c")
    attended_out = join_heads(core, attended, attended_other)

    holds, finished = [], []
    for members, exchanged, last in GROUPS:
        holds.append(place_bit(last) == core)
        finished += finish_group([reduced[p] for p in members], exchanged, last)
    kept, sent = sort_pieces(jnp.stack(holds).astype(jnp.int32), finished)
    received = swap(sent, "c")
    new_weights, new_first, new_second = adam(
        core, kept, received, weights_master, adam_first, adam_second
    )
    return (attended_out, new_weights, new_first, new_second)


def solution(mesh):
    torus = Mesh(mesh.devices.reshape(4, 4, 4, 2), ("x", "y", "z", "c"))
    rows = P(("z", "c"), ("x", "y"), None)
    shard = P(("z", "c"), None)
    return jax.shard_map(
        step,
        mesh=torus,
        in_specs=(rows, shard, shard, shard, rows),
        out_specs=(rows, shard, shard, shard),
        check_vma=False,
    )
```
